256 devices in a mesh: lon: 8 (over y_hi, x), lat: 32 (over z, y_lo, core).
Axes of the slice: x: 4, y: 4 (y_hi: 2, y_lo: 2; y = y_hi * 2 + y_lo), z: 8, core: 2. Of those that a mesh axis runs over, the one named last changes fastest.
Arguments:
- prognostic: bfloat16 [7, 8, 512, 4096], P(None, None, 'lat', 'lon'), may hold values from -6 to 6
- halo_depth: int32 [2, 32, 8], P(None, 'lat', 'lon'), may hold values from 3 to 10, as said below
- cell_offsets: int32 [2, 8, 512, 4096], P(None, None, 'lat', 'lon'), may hold values from -8 to 8, as said below
Outputs:
- advected: bfloat16 [7, 8, 512, 4096], P(None, None, 'lat', 'lon')
The draws below stay inside these ranges and needn't reach their ends.
Inputs may be any that keep to these rules, and one draw needn't show every extreme that they name: `halo_depth`: every depth is 3 or more; row depths are at most 10, column depths at most 8; some tile has row depth 10 and column depth 8. |cell_offsets[0]| <= (its tile's row depth) - 2 and |cell_offsets[1]| <= (its tile's column depth) - 2; row y + cell_offsets[0] lies in 0 to 510.
All inputs are finite; a program needn't handle non-finite values.
Results may differ from the reference program's by a relative error of at most 0.0047.
Values may be sent and summed in bfloat16 or wider, within the bound.
No kernel may reach another device: no remote copies, remote signals or barrier semaphores. Data moves between devices by JAX's collectives and lax.ppermute only.
A program may use at most 64 MiB of HBM per device.

```python
import math
import jax
import jax.numpy as jnp
from jax import lax

NFIELD = 7
LEV = 8
CLAT = 16
CLON = 512
HO = 8
HL = 10
ITERS = 3
NLAT = 512
NLON = 4096
N_LON = 8
N_LAT = 32


def depth_grid(key):
    base_key = jax.random.fold_in(key, 101)
    row_depths = jax.random.randint(jax.random.fold_in(base_key, 1), (N_LAT, N_LON), 3, HL + 1)
    col_depths = jax.random.randint(jax.random.fold_in(base_key, 2), (N_LAT, N_LON), 3, HO + 1)
    row_depths = row_depths.at[N_LAT // 2, 0].set(HL).at[0, 0].set(3)
    col_depths = col_depths.at[N_LAT // 2, 0].set(HO).at[0, 0].set(3)
    return jnp.stack([row_depths, col_depths]).astype(jnp.int32)


def draw_halo_depth(key, part):
    return depth_grid(key)


def draw_cell_offsets(key, part):
    grid_depth = depth_grid(key)
    rows_depth = jnp.repeat(jnp.repeat(grid_depth[0], CLAT, axis=0), CLON, axis=1)
    cols_depth = jnp.repeat(jnp.repeat(grid_depth[1], CLAT, axis=0), CLON, axis=1)
    lat_row = jnp.arange(NLAT, dtype=jnp.int32)[:, None]
    lat_low = jnp.maximum(2 - rows_depth, 0 - lat_row)
    lat_high = jnp.minimum(rows_depth - 2, NLAT - 2 - lat_row)
    grid_shape = (LEV, NLAT, NLON)
    row_off = jax.random.randint(jax.random.fold_in(key, 3), grid_shape, lat_low[None], lat_high[None] + 1)
    col_off = jax.random.randint(jax.random.fold_in(key, 4), grid_shape, 2 - cols_depth[None], cols_depth[None] - 1)
    centre = N_LAT // 2 * CLAT
    row_off = row_off.at[0, centre, 0].set(HL - 2).at[0, centre, 1].set(2 - HL)
    col_off = col_off.at[0, centre, 0].set(HO - 2).at[0, centre, 1].set(2 - HO)
    return jnp.stack([row_off, col_off]).astype(jnp.int32)


def levels(own_key, extent, split, least, high):
    gain, own = 1.0, jax.random.fold_in(own_key, 6)
    for position, parts in split:
        heights = jnp.exp(jax.random.uniform(jax.random.fold_in(own, position), (parts,), jnp.float32, least / len(split), high / len(split)))
        gain = gain * jnp.repeat(heights, extent[position] // parts).reshape([-1 if axis == position else 1 for axis in range(len(extent))])
    return gain


def bell_draw(rng, extent, scale, limit, cuts=(), kind=jnp.bfloat16):
    result = jax.random.normal(rng, extent, jnp.float32) * scale
    if len(cuts) > 0:
        result = levels(rng, extent, cuts, -0.22, 0.18) * result
    return jnp.clip(result, min=-limit, max=limit).astype(kind)


def setup_inputs(seed: int = 0) -> dict:
    streams_of = jax.random.split(jax.random.key(seed), 4)
    prognostic = bell_draw(streams_of[0], (NFIELD, LEV, NLAT, NLON), 1.0, 6.0, ((2, 32), (3, 8)))
    halo_depth = draw_halo_depth(jax.random.fold_in(streams_of[3], 71), 0)
    cell_offsets = draw_cell_offsets(jax.random.fold_in(streams_of[3], 71), 0)
    return dict(prognostic=prognostic, halo_depth=halo_depth, cell_offsets=cell_offsets)


courant = 2.0


def keys_kernel(offset):
    magnitude = jnp.abs(offset)
    near_part = (1.5 * magnitude - 2.5) * magnitude * magnitude + 1.0
    far_part = ((-0.5 * magnitude + 2.5) * magnitude - 4.0) * magnitude + 2.0
    return jnp.where(magnitude <= 1.0, near_part, jnp.where(magnitude < 2.0, far_part, 0.0))


def pad_fields(fields):
    wrapped = jnp.concatenate([fields[:, :, NLON - HO:], fields, fields[:, :, :HO]], axis=2)
    return jnp.pad(wrapped, ((0, 0), (HL, HL), (0, 0)))


def sample(padded, row_off, row_frac, col_off, col_frac):
    lat_rows = jnp.arange(NLAT, dtype=jnp.int32)[:, None] + (HL - 1) + row_off
    lon_cols = jnp.arange(NLON, dtype=jnp.int32)[None, :] + (HO - 1) + col_off
    summed = jnp.zeros((padded.shape[0], NLAT, NLON), jnp.float32)
    for row_tap in range(4):
        row_weight = keys_kernel((row_tap - 1.0) - row_frac)
        along = jnp.zeros((padded.shape[0], NLAT, NLON), jnp.float32)
        for col_tap in range(4):
            col_weight = keys_kernel((col_tap - 1.0) - col_frac).astype(jnp.bfloat16)
            col_weight = lax.optimization_barrier(col_weight).astype(jnp.float32)
            picked = padded[:, lat_rows + row_tap, lon_cols + col_tap].astype(jnp.float32)
            along = along + col_weight * picked
        summed = summed + row_weight * along
    return summed


def trajectory(wind_pad, row_off, col_off, rows_depth, cols_depth, coslat):
    row_frac = jnp.full(row_off.shape, 0.5, jnp.float32)
    col_frac = jnp.full(col_off.shape, 0.5, jnp.float32)
    row_mid = jnp.floor_divide(row_off, 2)
    col_mid = jnp.floor_divide(col_off, 2)
    row_float = row_off.astype(jnp.float32)
    col_float = col_off.astype(jnp.float32)
    for repeat in range(ITERS):
        row_part = ((row_off - 2 * row_mid).astype(jnp.float32) + row_frac) * 0.5
        col_part = ((col_off - 2 * col_mid).astype(jnp.float32) + col_frac) * 0.5
        mid_wind = sample(wind_pad, row_mid, row_part, col_mid, col_part)
        lon_reach = -courant * mid_wind[0] / coslat
        lat_reach = -courant * mid_wind[1]
        lon_limit = (cols_depth - 1.0) * jnp.tanh(lon_reach / (cols_depth - 1.0))
        lat_limit = (rows_depth - 1.0) * jnp.tanh(lat_reach / (rows_depth - 1.0))
        row_frac = 0.5 + 0.5 * jnp.tanh(0.5 * (lat_limit - row_float - 0.5))
        col_frac = 0.5 + 0.5 * jnp.tanh(0.5 * (lon_limit - col_float - 0.5))
    return row_frac, col_frac


def reference(prognostic, halo_depth, cell_offsets):
    rows_depth = jnp.repeat(jnp.repeat(halo_depth[0], CLAT, axis=0), CLON, axis=1).astype(jnp.float32)
    cols_depth = jnp.repeat(jnp.repeat(halo_depth[1], CLAT, axis=0), CLON, axis=1).astype(jnp.float32)
    lat_index = jnp.arange(NLAT, dtype=jnp.int32).astype(jnp.float32)
    coslat = jnp.cos((lat_index + 0.5) * (math.pi / NLAT) - 0.5 * math.pi)[:, None]

    def one_level(level_index):
        fields = lax.dynamic_index_in_dim(prognostic, level_index, 1, keepdims=False)
        offsets_level = lax.dynamic_index_in_dim(cell_offsets, level_index, 1, keepdims=False)
        padded = pad_fields(fields)
        row_off = offsets_level[0]
        col_off = offsets_level[1]
        row_frac, col_frac = trajectory(padded[0:2], row_off, col_off, rows_depth, cols_depth, coslat)
        return sample(padded, row_off, row_frac, col_off, col_frac).astype(jnp.bfloat16)

    advected = lax.map(one_level, jnp.arange(LEV, dtype=jnp.int32))
    return jnp.moveaxis(advected, 0, 1)
```

```python
import math

import jax
import jax.numpy as jnp
from jax import lax
from jax.experimental import pallas as pl
from jax.experimental.pallas import tpu as pltpu
from jax.sharding import PartitionSpec as P

HO = 8
HL = 10
ITERS = 3
WEST = 7
LANES = 128
F32 = jnp.float32
BF16 = jnp.bfloat16

courant = 2.0


def passed_along(value, axis, by):
    devices = lax.axis_size(axis)
    pairs = [(i, i + by) for i in range(devices) if 0 <= i + by < devices]
    return lax.ppermute(value, axis, pairs)


def from_behind(value, axis, steps):
    count = lax.axis_size(axis)
    pairs = [(source, (source + steps) % count) for source in range(count)]
    return lax.ppermute(value, axis, pairs)


def iota(shape, dim):
    return lax.broadcasted_iota(jnp.int32, shape, dim)


def cubic_weights(t):
    near = (1.5 * t - 2.5) * t * t + 1.0
    s = 1.0 - t
    first = -0.5 * t * s * s
    last = -0.5 * s * t * t
    third = (1.5 * s - 2.5) * s * s + 1.0
    return first, near, third, last


def edge_kernel(fields_ref, edge_west_ref, edge_east_ref, stage):
    channels, levels, rows, cols = fields_ref.shape
    stage[pl.ds(7, rows, stride=8), :] = jnp.zeros((rows, LANES), F32)
    group = iota((8, LANES), 1) // 8
    lane = iota((rows, LANES), 1)

    def pack_level(k, carry):
        for c in range(channels):
            first = pltpu.roll(fields_ref[c, k, :, :LANES].astype(F32), WEST, 1)
            last = pltpu.roll(fields_ref[c, k, :, cols - LANES :].astype(F32), WEST, 1)
            stage[pl.ds(c, rows, stride=8), :] = jnp.where(lane < WEST, last, first)
        west = jnp.zeros((8, LANES), F32)
        east = jnp.zeros((8, LANES), F32)
        for r in range(rows):
            row = stage[8 * r : 8 * r + 8, :]
            slot = rows - 1 - r
            east = jnp.where(group == slot, pltpu.roll(row, 8 * slot, 1), east)
            west = jnp.where(group == slot, pltpu.roll(row, (8 * slot - WEST) % LANES, 1), west)
        edge_west_ref[k] = west.astype(BF16)
        edge_east_ref[k] = east.astype(BF16)
        return carry

    lax.fori_loop(0, levels, pack_level, 0)


def pack_kernel(fields_ref, own_ref, down_ref, up_ref, stage):
    channels, levels, rows, cols = fields_ref.shape
    for t in range(cols // LANES):
        stage[t, pl.ds(7, rows, stride=8), :] = jnp.zeros((rows, LANES), F32)

    def pack_level(k, carry):
        for c in range(channels):
            turned = pltpu.roll(fields_ref[c, k].astype(F32), WEST, 1)
            for t in range(cols // LANES):
                stage[t, pl.ds(c, rows, stride=8), :] = turned[:, LANES * t : LANES * (t + 1)]
        for t in range(cols // LANES):
            cc = slice(LANES * t, LANES * (t + 1))
            own_ref[k, :, cc] = stage[t].astype(BF16)
            down_ref[k, :, cc] = stage[t, (rows - HL) * 8 :, :].astype(BF16)
            up_ref[k, :, cc] = stage[t, : HL * 8, :].astype(BF16)
        return carry

    lax.fori_loop(0, levels, pack_level, 0)


def fill_band_tables(mask, lane_pos):
    offset = iota(mask.shape, 0) - (iota(mask.shape, 1) & (LANES - 1))
    mask[...] = jnp.where((offset >= 0) & (offset < 16), 1.0, 0.0).astype(BF16)
    lane_pos[...] = ((iota(lane_pos.shape, 0) - iota(lane_pos.shape, 1)) & 15).astype(F32)


def band_matrix(compact, mask):
    tiles = [compact * mask[16 * t : 16 * t + 16, :] for t in range(9)]
    tiles.append(jnp.zeros((112, 256), BF16))
    return jnp.concatenate(tiles, axis=0)


def track_kernel(
    wind_ref, above_ref, below_ref, west_ref, east_ref, cells_ref, param_ref,
    row_frac_ref, col_frac_ref,
    stage, spread, mask, lane_pos, dense, taps,
):
    _, levels, rows, cols = wind_ref.shape
    fill_band_tables(mask, lane_pos)

    def edge(west, east, c, first, count):
        def tall(packed, shift):
            parts = []
            for h in range(2):
                part = jnp.broadcast_to(packed[c : c + 1, :].astype(F32), (8, LANES))
                part = pltpu.roll(part, shift + 64 * h, 1)
                parts.append(pltpu.roll(part, 0, 1, stride=8, stride_axis=0))
            return jnp.concatenate(parts, axis=0)

        lane = iota((16, LANES), 1)
        return jnp.where(lane < WEST, tall(west, 8), tall(east, 8 + WEST))[first : first + count]

    def track_level(k, carry):
        lane = iota((32, LANES), 1)
        for c in range(2):
            above = above_ref[k, 8 * c : 8 * c + 8, :].astype(F32)
            below = below_ref[k, 8 * c : 8 * c + 8, :].astype(F32)
            own = wind_ref[c, k].astype(F32)
            turned = pltpu.roll(jnp.concatenate([above, own, below], axis=0), WEST, 1)
            halo = jnp.concatenate(
                [
                    edge(above_ref[k, 16:24, :LANES], above_ref[k, 16:24, LANES : 2 * LANES], c, 8, 8),
                    edge(west_ref[k], east_ref[k], c, 0, 16),
                    edge(below_ref[k, 16:24, :LANES], below_ref[k, 16:24, LANES : 2 * LANES], c, 0, 8),
                ],
                axis=0,
            )
            first = turned[:, :LANES]
            extended = jnp.concatenate(
                [
                    jnp.where(lane < WEST, halo, first),
                    turned[:, LANES:],
                    jnp.where(lane < WEST, first, jnp.where(lane < 15, halo, 0.0)),
                ],
                axis=1,
            )
            for b in range(4):
                moved = extended if b == 0 else pltpu.roll(extended, cols + LANES - b, 1)
                for t in range(cols // LANES + 1):
                    stage[t, pl.ds(2 * b + c, 32, stride=8), :] = moved[:, LANES * t : LANES * (t + 1)]
        for t in range(cols // LANES + 1):
            spread[:, LANES * t : LANES * (t + 1)] = stage[t].astype(BF16)

        row_off = cells_ref[0, k]
        col_off = cells_ref[1, k]
        row_mid = row_off >> 1
        col_mid = col_off >> 1
        for t in range(cols // LANES):
            dense[t, 0:16, :] = (col_mid[:, LANES * t : LANES * (t + 1)] + 6).astype(F32)
            dense[t, 16:32, :] = (row_mid[:, LANES * t : LANES * (t + 1)] + 4).astype(F32)

        def gather(pair, carry):
            y = 2 * pair
            start = pl.multiple_of(16 * pair + 16, 16)
            for block in range(cols // LANES):
                lo = block * LANES
                halves = []
                for n in range(2):
                    at = dense[block, pl.ds(y + n, 8, stride=0), :]
                    at = jnp.concatenate([at, at], axis=0)
                    halves.append(jnp.where(lane_pos[...] == at, 1.0, 0.0))
                compact = jnp.concatenate(halves, axis=1).astype(BF16)
                found = jnp.dot(
                    spread[pl.ds(start, 112), lo : lo + 256],
                    band_matrix(compact, mask),
                    preferred_element_type=F32,
                )
                for n in range(2):
                    depth = dense[block, pl.ds(16 + y + n, 8, stride=0), :]
                    v = [
                        found[8 * (1 + n + i) : 8 * (2 + n + i), n * LANES : (n + 1) * LANES]
                        for i in range(12)
                    ]
                    whole = depth >= 8.0
                    v = [jnp.where(whole, v[i + 8], v[i]) for i in range(4)] + v[4:]
                    depth = jnp.where(whole, depth - 8.0, depth)
                    for step, count in ((4, 7), (2, 5), (1, 4)):
                        far = depth >= float(step)
                        v = [jnp.where(far, v[i + step], v[i]) for i in range(count)]
                        depth = jnp.where(far, depth - float(step), depth)
                    for a in range(4):
                        taps[block, pl.ds(a * 136 + y + n, 8, stride=17), :] = v[a]
            return carry

        lax.fori_loop(0, rows // 2, gather, 0, unroll=True)

        for half in range(rows // 8):
            for tile in range(cols // LANES):
                rr = slice(8 * half, 8 * half + 8)
                cc = slice(LANES * tile, LANES * tile + LANES)
                cy = param_ref[16:24, :]
                dy = param_ref[24:32, :]
                dx = param_ref[32:40, :]
                cx = param_ref[rr, :]
                oy = row_off[rr, cc]
                ox = col_off[rr, cc]
                y_odd = (oy & 1).astype(F32)
                x_odd = (ox & 1).astype(F32)
                oyf = oy.astype(F32) + 0.5
                oxf = ox.astype(F32) + 0.5
                fy = jnp.full((8, LANES), 0.5, F32)
                fx = fy
                for _ in range(ITERS):
                    wy = cubic_weights((y_odd + fy) * 0.5)
                    wx = [w.astype(BF16).astype(F32) for w in cubic_weights((x_odd + fx) * 0.5)]
                    mid = []
                    for c in range(2):
                        total = None
                        for a in range(4):
                            along = None
                            for b in range(4):
                                base = a * 136 + (2 * b + c) * 17 + 8 * half
                                term = wx[b] * taps[tile, base : base + 8, :]
                                along = term if along is None else along + term
                            along = wy[a] * along
                            total = along if total is None else total + along
                        mid.append(total)
                    lx = dx * jnp.tanh(mid[0] * cx)
                    ly = dy * jnp.tanh(mid[1] * cy)
                    fy = 0.5 + 0.5 * jnp.tanh(0.5 * (ly - oyf))
                    fx = 0.5 + 0.5 * jnp.tanh(0.5 * (lx - oxf))
                row_frac_ref[k, rr, cc] = fy
                col_frac_ref[k, rr, cc] = fx
        return carry

    lax.fori_loop(0, levels, track_level, 0)


def advect_kernel(
    own_ref, above_ref, below_ref, west_ref, east_ref, far_above_ref, far_below_ref, cells_ref,
    row_frac_ref, col_frac_ref,
    out_ref,
    spread, mask, lane_pos, dense, result,
):
    channels, levels, rows, cols = out_ref.shape
    fill_band_tables(mask, lane_pos)

    def place(block, west, east, first, count, at):
        west = west.astype(F32)
        east = east.astype(F32)
        halo = []
        lane = iota((8, LANES), 1)
        for r in range(first, first + count):
            a = pltpu.roll(west, (8 * r + 8) % LANES, 1)
            b = pltpu.roll(east, (8 * r + 8 + WEST) % LANES, 1)
            halo.append(jnp.where(lane < WEST, a, jnp.where(lane < 15, b, 0.0)))
        halo = jnp.concatenate(halo, axis=0)
        lanes = iota((8 * count, LANES), 1)
        start = block[:, :LANES].astype(F32)
        spread[at : at + 8 * count, :LANES] = jnp.where(lanes < WEST, halo, start).astype(BF16)
        spread[at : at + 8 * count, LANES:cols] = block[:, LANES:]
        spread[at : at + 8 * count, cols:] = jnp.where(lanes < WEST, start, halo).astype(BF16)

    def advect_level(k, carry):
        place(above_ref[k], far_above_ref[k, 16:24, :LANES], far_above_ref[k, 16:24, LANES : 2 * LANES], rows - HL, HL, 0)
        place(own_ref[k], west_ref[k], east_ref[k], 0, rows, 8 * HL)
        place(below_ref[k], far_below_ref[k, 16:24, :LANES], far_below_ref[k, 16:24, LANES : 2 * LANES], 0, HL, 8 * (HL + rows))

        for t in range(cols // LANES):
            cc = slice(LANES * t, LANES * (t + 1))
            dense[t, 0:16, :] = (cells_ref[1, k, :, cc] + 6).astype(F32)
            dense[t, 16:32, :] = (cells_ref[0, k, :, cc] + 8).astype(F32)
            for i, w in enumerate(cubic_weights(col_frac_ref[k, :, cc])):
                dense[t, 32 + 16 * i : 48 + 16 * i, :] = w.astype(BF16).astype(F32)
            for i, w in enumerate(cubic_weights(row_frac_ref[k, :, cc])):
                dense[t, 96 + 16 * i : 112 + 16 * i, :] = w

        def sample(pair, carry):
            y = 2 * pair
            start = pl.multiple_of(16 * pair, 16)
            for block in range(cols // LANES):
                lo = block * LANES
                halves = []
                for n in range(2):
                    def wide(part):
                        return dense[block, pl.ds(16 * part + y + n, 8, stride=0), :]

                    at = wide(0)
                    w = [wide(2 + b) for b in range(4)]
                    both = []
                    for h in range(2):
                        rel = lane_pos[8 * h : 8 * h + 8, :] - at
                        picked = jnp.where(rel == 3.0, w[3], 0.0)
                        picked = jnp.where(rel == 2.0, w[2], picked)
                        picked = jnp.where(rel == 1.0, w[1], picked)
                        both.append(jnp.where(rel == 0.0, w[0], picked))
                    halves.append(jnp.concatenate(both, axis=0))
                compact = jnp.concatenate(halves, axis=1).astype(BF16)
                mixed = jnp.dot(
                    spread[pl.ds(start, 176), lo : lo + 256],
                    band_matrix(compact, mask),
                    preferred_element_type=F32,
                )
                for n in range(2):
                    depth = dense[block, pl.ds(16 + y + n, 8, stride=0), :]
                    v = [
                        mixed[8 * (1 + n + i) : 8 * (2 + n + i), n * LANES : (n + 1) * LANES]
                        for i in range(20)
                    ]
                    whole = depth >= 16.0
                    v = [jnp.where(whole, v[i + 16], v[i]) for i in range(4)] + v[4:]
                    depth = jnp.where(whole, depth - 16.0, depth)
                    for step, count in ((8, 11), (4, 7), (2, 5), (1, 4)):
                        far = depth >= float(step)
                        v = [jnp.where(far, v[i + step], v[i]) for i in range(count)]
                        depth = jnp.where(far, depth - float(step), depth)
                    total = None
                    for a in range(4):
                        weight = dense[block, pl.ds(96 + 16 * a + y + n, 8, stride=0), :]
                        total = weight * v[a] if total is None else total + weight * v[a]
                    result[block, pl.ds(y + n, 8, stride=17), :] = total
            return carry

        lax.fori_loop(0, rows // 2, sample, 0, unroll=True)
        for c in range(channels):
            for t in range(cols // LANES):
                cc = slice(LANES * t, LANES * (t + 1))
                out_ref[c, k, :, cc] = result[t, 17 * c : 17 * c + 16, :].astype(BF16)
        return carry

    lax.fori_loop(0, levels, advect_level, 0)


def call(kernel, outs, scratch, args, name, flops):
    moved = sum(a.size * a.dtype.itemsize for a in list(args) + list(outs))
    in_vmem = pl.BlockSpec(memory_space=pltpu.VMEM)
    return pl.pallas_call(
        kernel,
        in_specs=[in_vmem] * len(args),
        out_specs=[in_vmem] * len(outs),
        out_shape=outs,
        scratch_shapes=scratch,
        cost_estimate=pl.CostEstimate(flops=flops, bytes_accessed=moved, transcendentals=0),
        compiler_params=pltpu.CompilerParams(vmem_limit_bytes=24 << 20),
        name=name,
    )(*args)


def on_device(prognostic, halo_depth, cell_offsets):
    channels, levels, rows, cols = prognostic.shape
    tiles = cols // LANES
    shape = jax.ShapeDtypeStruct
    edge = shape((levels, 8, LANES), BF16)
    edge_west, edge_east = call(
        edge_kernel, [edge, edge], [pltpu.VMEM((8 * rows, LANES), F32)], [prognostic], "edge", 10**6
    )
    west = from_behind(edge_east, "lon", 1)
    east = from_behind(edge_west, "lon", -1)
    own, down, up = call(
        pack_kernel,
        [shape((levels, 8 * n, cols), BF16) for n in (rows, HL, HL)],
        [pltpu.VMEM((tiles, 8 * rows, LANES), F32)],
        [prognostic], "pack", 10**6,
    )

    lat_total = rows * lax.axis_size("lat")
    lat_index = (lax.axis_index("lat") * rows + jnp.arange(rows, dtype=jnp.int32)).astype(F32)
    coslat = jnp.cos((lat_index + 0.5) * (math.pi / lat_total) - 0.5 * math.pi)
    reach = halo_depth[:, 0, 0].astype(F32) - 1.0
    params = jnp.concatenate(
        [-courant / (coslat * reach[1]), jnp.repeat(jnp.stack([-courant / reach[0], reach[0], reach[1]]), 8)]
    )
    params = jnp.broadcast_to(params[:, None], (rows + 24, LANES))

    edges = jnp.concatenate([west, east, jnp.zeros((levels, 8, cols - 2 * LANES), BF16)], axis=2)
    send_down = jnp.concatenate([prognostic[0, :, rows - 8 :], prognostic[1, :, rows - 8 :], edges], axis=1)
    send_up = jnp.concatenate([prognostic[0, :, :8], prognostic[1, :, :8], edges], axis=1)
    send_down, send_up, params = lax.optimization_barrier((send_down, send_up, params))
    far_above = passed_along(send_down, "lat", 1)
    far_below = passed_along(send_up, "lat", -1)
    far_above, far_below, down, up = lax.optimization_barrier((far_above, far_below, down, up))
    above = passed_along(down, "lat", 1)
    below = passed_along(up, "lat", -1)

    frac = shape((levels, rows, cols), F32)
    row_frac, col_frac = call(
        track_kernel,
        [frac, frac],
        [
            pltpu.VMEM((tiles + 1, 8 * 32, LANES), F32),
            pltpu.VMEM((8 * 32, cols + LANES), BF16),
            pltpu.VMEM((144, 256), BF16),
            pltpu.VMEM((16, LANES), F32),
            pltpu.VMEM((tiles, 32, LANES), F32),
            pltpu.VMEM((tiles, 4 * 136, LANES), F32),
        ],
        [prognostic, far_above, far_below, west, east, cell_offsets, params],
        "track", 40 * 10**6,
    )
    return call(
        advect_kernel,
        [shape(prognostic.shape, BF16)],
        [
            pltpu.VMEM((8 * (rows + 2 * HL), cols + LANES), BF16),
            pltpu.VMEM((144, 256), BF16),
            pltpu.VMEM((16, LANES), F32),
            pltpu.VMEM((tiles, 160, LANES), F32),
            pltpu.VMEM((tiles, 136, LANES), F32),
        ],
        [own, above, below, west, east, far_above, far_below, cell_offsets, row_frac, col_frac],
        "advect", 40 * 10**6,
    )[0]


def solution(mesh):
    in_specs = (P(None, None, "lat", "lon"), P(None, "lat", "lon"), P(None, None, "lat", "lon"))
    out_specs = P(None, None, "lat", "lon")
    return jax.shard_map(
        on_device, mesh=mesh, in_specs=in_specs, out_specs=out_specs, check_vma=False
    )
```

```python
import math

import jax
import jax.numpy as jnp
from jax import lax
from jax.experimental import pallas as pl
from jax.experimental.pallas import tpu as pltpu
from jax.sharding import PartitionSpec as P

HO = 8
HL = 10
ITERS = 3
NEAR = 8
FAR = HL - NEAR
WEST = 7
LANES = 128
F32 = jnp.float32
BF16 = jnp.bfloat16

courant = 2.0


def passed_along(value, axis, by):
    devices = lax.axis_size(axis)
    pairs = [(i, i + by) for i in range(devices) if 0 <= i + by < devices]
    return lax.ppermute(value, axis, pairs)


def from_behind(value, axis, steps):
    count = lax.axis_size(axis)
    pairs = [(source, (source + steps) % count) for source in range(count)]
    return lax.ppermute(value, axis, pairs)


def iota(shape, dim):
    return lax.broadcasted_iota(jnp.int32, shape, dim)


def cubic_weights(t):
    near = (1.5 * t - 2.5) * t * t + 1.0
    s = 1.0 - t
    first = -0.5 * t * s * s
    last = -0.5 * s * t * t
    third = (1.5 * s - 2.5) * s * s + 1.0
    return first, near, third, last


def edge_kernel(fields_ref, edge_west_ref, edge_east_ref, stage):
    channels, levels, rows, cols = fields_ref.shape
    stage[pl.ds(7, rows, stride=8), :] = jnp.zeros((rows, LANES), F32)
    group = iota((8, LANES), 1) // 8
    lane = iota((rows, LANES), 1)

    def pack_level(k, carry):
        for c in range(channels):
            first = pltpu.roll(fields_ref[c, k, :, :LANES].astype(F32), WEST, 1)
            last = pltpu.roll(fields_ref[c, k, :, cols - LANES :].astype(F32), WEST, 1)
            stage[pl.ds(c, rows, stride=8), :] = jnp.where(lane < WEST, last, first)
        west = jnp.zeros((8, LANES), F32)
        east = jnp.zeros((8, LANES), F32)
        for r in range(rows):
            row = stage[8 * r : 8 * r + 8, :]
            slot = rows - 1 - r
            east = jnp.where(group == slot, pltpu.roll(row, 8 * slot, 1), east)
            west = jnp.where(group == slot, pltpu.roll(row, (8 * slot - WEST) % LANES, 1), west)
        edge_west_ref[k] = west.astype(BF16)
        edge_east_ref[k] = east.astype(BF16)
        return carry

    lax.fori_loop(0, levels, pack_level, 0)


def to_row_major(fields_ref, k, stage):
    channels, _, rows, cols = fields_ref.shape
    for c in range(channels):
        turned = pltpu.roll(fields_ref[c, k].astype(F32), WEST, 1)
        for t in range(cols // LANES):
            stage[t, pl.ds(c, rows, stride=8), :] = turned[:, LANES * t : LANES * (t + 1)]


def clear_last_field(stage, rows):
    for t in range(stage.shape[0]):
        stage[t, pl.ds(7, rows, stride=8), :] = jnp.zeros((rows, LANES), F32)


def pack_kernel(fields_ref, own_ref, down_ref, up_ref, stage):
    _, levels, rows, cols = fields_ref.shape
    clear_last_field(stage, rows)
    down, up = 8 * (rows - HL), 8 * NEAR

    def pack_level(k, carry):
        to_row_major(fields_ref, k, stage)
        for t in range(cols // LANES):
            cc = slice(LANES * t, LANES * (t + 1))
            own_ref[k, :, cc] = stage[t].astype(BF16)
            down_ref[k, :, cc] = stage[t, down : down + 8 * FAR, :].astype(BF16)
            up_ref[k, :, cc] = stage[t, up : up + 8 * FAR, :].astype(BF16)
        return carry

    lax.fori_loop(0, levels, pack_level, 0)


def relay_kernel(above_ref, below_ref, above_out, below_out, stage, other):
    _, levels, rows, cols = above_ref.shape
    clear_last_field(stage, rows)
    clear_last_field(other, rows)

    def relay_level(k, carry):
        to_row_major(above_ref, k, stage)
        to_row_major(below_ref, k, other)
        for t in range(cols // LANES):
            cc = slice(LANES * t, LANES * (t + 1))
            above_out[k, :, cc] = stage[t].astype(BF16)
            below_out[k, :, cc] = other[t].astype(BF16)
        return carry

    lax.fori_loop(0, levels, relay_level, 0)


def fill_band_tables(mask, lane_pos):
    offset = iota(mask.shape, 0) - (iota(mask.shape, 1) & (LANES - 1))
    mask[...] = jnp.where((offset >= 0) & (offset < 16), 1.0, 0.0).astype(BF16)
    lane_pos[...] = ((iota(lane_pos.shape, 0) - iota(lane_pos.shape, 1)) & 15).astype(F32)


def band_matrix(compact, mask):
    tiles = [compact * mask[16 * t : 16 * t + 16, :] for t in range(9)]
    tiles.append(jnp.zeros((112, 256), BF16))
    return jnp.concatenate(tiles, axis=0)


def track_kernel(
    wind_ref, above_ref, below_ref, far_above_ref, far_below_ref, west_ref, east_ref, cells_ref, param_ref,
    row_frac_ref, col_frac_ref,
    stage, spread, mask, lane_pos, dense, taps,
):
    _, levels, rows, cols = wind_ref.shape
    fill_band_tables(mask, lane_pos)

    def edge(west, east, c, first, count):
        def tall(packed, shift):
            parts = []
            for h in range(2):
                part = jnp.broadcast_to(packed[c : c + 1, :].astype(F32), (8, LANES))
                part = pltpu.roll(part, shift + 64 * h, 1)
                parts.append(pltpu.roll(part, 0, 1, stride=8, stride_axis=0))
            return jnp.concatenate(parts, axis=0)

        lane = iota((16, LANES), 1)
        return jnp.where(lane < WEST, tall(west, 8), tall(east, 8 + WEST))[first : first + count]

    def track_level(k, carry):
        lane = iota((32, LANES), 1)
        for c in range(2):
            above = above_ref[c, k].astype(F32)
            below = below_ref[c, k].astype(F32)
            own = wind_ref[c, k].astype(F32)
            turned = pltpu.roll(jnp.concatenate([above, own, below], axis=0), WEST, 1)
            halo = jnp.concatenate(
                [
                    edge(far_above_ref[k, 16:24, :LANES], far_above_ref[k, 16:24, LANES : 2 * LANES], c, 8, 8),
                    edge(west_ref[k], east_ref[k], c, 0, 16),
                    edge(far_below_ref[k, 16:24, :LANES], far_below_ref[k, 16:24, LANES : 2 * LANES], c, 0, 8),
                ],
                axis=0,
            )
            first = turned[:, :LANES]
            extended = jnp.concatenate(
                [
                    jnp.where(lane < WEST, halo, first),
                    turned[:, LANES:],
                    jnp.where(lane < WEST, first, jnp.where(lane < 15, halo, 0.0)),
                ],
                axis=1,
            )
            for b in range(4):
                moved = extended if b == 0 else pltpu.roll(extended, cols + LANES - b, 1)
                for t in range(cols // LANES + 1):
                    stage[t, pl.ds(2 * b + c, 32, stride=8), :] = moved[:, LANES * t : LANES * (t + 1)]
        for t in range(cols // LANES + 1):
            spread[:, LANES * t : LANES * (t + 1)] = stage[t].astype(BF16)

        row_off = cells_ref[0, k]
        col_off = cells_ref[1, k]
        row_mid = row_off >> 1
        col_mid = col_off >> 1
        for t in range(cols // LANES):
            dense[t, 0:16, :] = (col_mid[:, LANES * t : LANES * (t + 1)] + 6).astype(F32)
            dense[t, 16:32, :] = (row_mid[:, LANES * t : LANES * (t + 1)] + 4).astype(F32)

        def gather(pair, carry):
            y = 2 * pair
            start = pl.multiple_of(16 * pair + 16, 16)
            for block in range(cols // LANES):
                lo = block * LANES
                halves = []
                for n in range(2):
                    at = dense[block, pl.ds(y + n, 8, stride=0), :]
                    at = jnp.concatenate([at, at], axis=0)
                    halves.append(jnp.where(lane_pos[...] == at, 1.0, 0.0))
                compact = jnp.concatenate(halves, axis=1).astype(BF16)
                found = jnp.dot(
                    spread[pl.ds(start, 112), lo : lo + 256],
                    band_matrix(compact, mask),
                    preferred_element_type=F32,
                )
                for n in range(2):
                    depth = dense[block, pl.ds(16 + y + n, 8, stride=0), :]
                    v = [
                        found[8 * (1 + n + i) : 8 * (2 + n + i), n * LANES : (n + 1) * LANES]
                        for i in range(12)
                    ]
                    whole = depth >= 8.0
                    v = [jnp.where(whole, v[i + 8], v[i]) for i in range(4)] + v[4:]
                    depth = jnp.where(whole, depth - 8.0, depth)
                    for step, count in ((4, 7), (2, 5), (1, 4)):
                        far = depth >= float(step)
                        v = [jnp.where(far, v[i + step], v[i]) for i in range(count)]
                        depth = jnp.where(far, depth - float(step), depth)
                    for a in range(4):
                        taps[block, pl.ds(a * 136 + y + n, 8, stride=17), :] = v[a]
            return carry

        lax.fori_loop(0, rows // 2, gather, 0, unroll=True)

        for half in range(rows // 8):
            for tile in range(cols // LANES):
                rr = slice(8 * half, 8 * half + 8)
                cc = slice(LANES * tile, LANES * tile + LANES)
                cy = param_ref[16:24, :]
                dy = param_ref[24:32, :]
                dx = param_ref[32:40, :]
                cx = param_ref[rr, :]
                oy = row_off[rr, cc]
                ox = col_off[rr, cc]
                y_odd = (oy & 1).astype(F32)
                x_odd = (ox & 1).astype(F32)
                oyf = oy.astype(F32) + 0.5
                oxf = ox.astype(F32) + 0.5
                fy = jnp.full((8, LANES), 0.5, F32)
                fx = fy
                for _ in range(ITERS):
                    wy = cubic_weights((y_odd + fy) * 0.5)
                    wx = [w.astype(BF16).astype(F32) for w in cubic_weights((x_odd + fx) * 0.5)]
                    mid = []
                    for c in range(2):
                        total = None
                        for a in range(4):
                            along = None
                            for b in range(4):
                                base = a * 136 + (2 * b + c) * 17 + 8 * half
                                term = wx[b] * taps[tile, base : base + 8, :]
                                along = term if along is None else along + term
                            along = wy[a] * along
                            total = along if total is None else total + along
                        mid.append(total)
                    lx = dx * jnp.tanh(mid[0] * cx)
                    ly = dy * jnp.tanh(mid[1] * cy)
                    fy = 0.5 + 0.5 * jnp.tanh(0.5 * (ly - oyf))
                    fx = 0.5 + 0.5 * jnp.tanh(0.5 * (lx - oxf))
                row_frac_ref[k, rr, cc] = fy
                col_frac_ref[k, rr, cc] = fx
        return carry

    lax.fori_loop(0, levels, track_level, 0)


def advect_kernel(
    own_ref, above_ref, below_ref, west_ref, east_ref, far_above_ref, far_below_ref, cells_ref,
    row_frac_ref, col_frac_ref,
    out_ref,
    spread, mask, lane_pos, dense, result,
):
    channels, levels, rows, cols = out_ref.shape
    fill_band_tables(mask, lane_pos)

    def place(block, west, east, first, count, at):
        west = west.astype(F32)
        east = east.astype(F32)
        halo = []
        lane = iota((8, LANES), 1)
        for r in range(first, first + count):
            a = pltpu.roll(west, (8 * r + 8) % LANES, 1)
            b = pltpu.roll(east, (8 * r + 8 + WEST) % LANES, 1)
            halo.append(jnp.where(lane < WEST, a, jnp.where(lane < 15, b, 0.0)))
        halo = jnp.concatenate(halo, axis=0)
        lanes = iota((8 * count, LANES), 1)
        start = block[:, :LANES].astype(F32)
        spread[at : at + 8 * count, :LANES] = jnp.where(lanes < WEST, halo, start).astype(BF16)
        spread[at : at + 8 * count, LANES:cols] = block[:, LANES:]
        spread[at : at + 8 * count, cols:] = jnp.where(lanes < WEST, start, halo).astype(BF16)

    def advect_level(k, carry):
        a_west, a_east = far_above_ref[k, 16:24, :LANES], far_above_ref[k, 16:24, LANES : 2 * LANES]
        b_west, b_east = far_below_ref[k, 16:24, :LANES], far_below_ref[k, 16:24, LANES : 2 * LANES]
        place(far_above_ref[k, : 8 * FAR, :], a_west, a_east, rows - HL, FAR, 0)
        place(above_ref[k], a_west, a_east, rows - NEAR, NEAR, 8 * FAR)
        place(own_ref[k], west_ref[k], east_ref[k], 0, rows, 8 * HL)
        place(below_ref[k], b_west, b_east, 0, NEAR, 8 * (HL + rows))
        place(far_below_ref[k, : 8 * FAR, :], b_west, b_east, NEAR, FAR, 8 * (HL + rows + NEAR))
        for t in range(cols // LANES):
            cc = slice(LANES * t, LANES * (t + 1))
            dense[t, 0:16, :] = (cells_ref[1, k, :, cc] + 6).astype(F32)
            dense[t, 16:32, :] = (cells_ref[0, k, :, cc] + 8).astype(F32)
            for i, w in enumerate(cubic_weights(col_frac_ref[k, :, cc])):
                dense[t, 32 + 16 * i : 48 + 16 * i, :] = w.astype(BF16).astype(F32)
            for i, w in enumerate(cubic_weights(row_frac_ref[k, :, cc])):
                dense[t, 96 + 16 * i : 112 + 16 * i, :] = w

        def sample(pair, carry):
            y = 2 * pair
            start = pl.multiple_of(16 * pair, 16)
            for block in range(cols // LANES):
                lo = block * LANES
                halves = []
                for n in range(2):
                    def wide(part):
                        return dense[block, pl.ds(16 * part + y + n, 8, stride=0), :]

                    at = wide(0)
                    w = [wide(2 + b) for b in range(4)]
                    both = []
                    for h in range(2):
                        rel = lane_pos[8 * h : 8 * h + 8, :] - at
                        picked = jnp.where(rel == 3.0, w[3], 0.0)
                        picked = jnp.where(rel == 2.0, w[2], picked)
                        picked = jnp.where(rel == 1.0, w[1], picked)
                        both.append(jnp.where(rel == 0.0, w[0], picked))
                    halves.append(jnp.concatenate(both, axis=0))
                compact = jnp.concatenate(halves, axis=1).astype(BF16)
                mixed = jnp.dot(
                    spread[pl.ds(start, 176), lo : lo + 256],
                    band_matrix(compact, mask),
                    preferred_element_type=F32,
                )
                for n in range(2):
                    depth = dense[block, pl.ds(16 + y + n, 8, stride=0), :]
                    v = [
                        mixed[8 * (1 + n + i) : 8 * (2 + n + i), n * LANES : (n + 1) * LANES]
                        for i in range(20)
                    ]
                    whole = depth >= 16.0
                    v = [jnp.where(whole, v[i + 16], v[i]) for i in range(4)] + v[4:]
                    depth = jnp.where(whole, depth - 16.0, depth)
                    for step, count in ((8, 11), (4, 7), (2, 5), (1, 4)):
                        far = depth >= float(step)
                        v = [jnp.where(far, v[i + step], v[i]) for i in range(count)]
                        depth = jnp.where(far, depth - float(step), depth)
                    total = None
                    for a in range(4):
                        weight = dense[block, pl.ds(96 + 16 * a + y + n, 8, stride=0), :]
                        total = weight * v[a] if total is None else total + weight * v[a]
                    result[block, pl.ds(y + n, 8, stride=17), :] = total
            return carry

        lax.fori_loop(0, rows // 2, sample, 0, unroll=True)
        for c in range(channels):
            for t in range(cols // LANES):
                cc = slice(LANES * t, LANES * (t + 1))
                out_ref[c, k, :, cc] = result[t, 17 * c : 17 * c + 16, :].astype(BF16)
        return carry

    lax.fori_loop(0, levels, advect_level, 0)


def call(kernel, outs, scratch, args, name, flops):
    moved = sum(a.size * a.dtype.itemsize for a in list(args) + list(outs))
    in_vmem = pl.BlockSpec(memory_space=pltpu.VMEM)
    return pl.pallas_call(
        kernel,
        in_specs=[in_vmem] * len(args),
        out_specs=[in_vmem] * len(outs),
        out_shape=outs,
        scratch_shapes=scratch,
        cost_estimate=pl.CostEstimate(flops=flops, bytes_accessed=moved, transcendentals=0),
        compiler_params=pltpu.CompilerParams(vmem_limit_bytes=24 << 20),
        name=name,
    )(*args)


def on_device(prognostic, halo_depth, cell_offsets):
    channels, levels, rows, cols = prognostic.shape
    tiles = cols // LANES
    shape = jax.ShapeDtypeStruct
    above = passed_along(prognostic[:, :, rows - NEAR :], "lat", 1)
    below = passed_along(prognostic[:, :, :NEAR], "lat", -1)
    edge = shape((levels, 8, LANES), BF16)
    edge_west, edge_east = call(
        edge_kernel, [edge, edge], [pltpu.VMEM((8 * rows, LANES), F32)], [prognostic], "edge", 10**6
    )
    west = from_behind(edge_east, "lon", 1)
    east = from_behind(edge_west, "lon", -1)
    own, down, up = call(
        pack_kernel,
        [shape((levels, 8 * n, cols), BF16) for n in (rows, FAR, FAR)],
        [pltpu.VMEM((tiles, 8 * rows, LANES), F32)],
        [prognostic], "pack", 10**6,
    )

    lat_total = rows * lax.axis_size("lat")
    lat_index = (lax.axis_index("lat") * rows + jnp.arange(rows, dtype=jnp.int32)).astype(F32)
    coslat = jnp.cos((lat_index + 0.5) * (math.pi / lat_total) - 0.5 * math.pi)
    reach = halo_depth[:, 0, 0].astype(F32) - 1.0
    params = jnp.concatenate(
        [-courant / (coslat * reach[1]), jnp.repeat(jnp.stack([-courant / reach[0], reach[0], reach[1]]), 8)]
    )
    params = jnp.broadcast_to(params[:, None], (rows + 24, LANES))

    edges = jnp.concatenate([west, east, jnp.zeros((levels, 8, cols - 2 * LANES), BF16)], axis=2)
    send_down = jnp.concatenate([down, edges], axis=1)
    send_up = jnp.concatenate([up, edges], axis=1)
    send_down, send_up, params = lax.optimization_barrier((send_down, send_up, params))
    far_above = passed_along(send_down, "lat", 1)
    far_below = passed_along(send_up, "lat", -1)
    halo = shape((levels, 8 * NEAR, cols), BF16)
    relayed_above, relayed_below = call(
        relay_kernel, [halo, halo], [pltpu.VMEM((tiles, 8 * NEAR, LANES), F32)] * 2,
        [above, below], "relay", 10**6,
    )
    relayed_above, relayed_below, far_above, far_below = lax.optimization_barrier(
        (relayed_above, relayed_below, far_above, far_below)
    )

    frac = shape((levels, rows, cols), F32)
    row_frac, col_frac = call(
        track_kernel,
        [frac, frac],
        [
            pltpu.VMEM((tiles + 1, 8 * 32, LANES), F32),
            pltpu.VMEM((8 * 32, cols + LANES), BF16),
            pltpu.VMEM((144, 256), BF16),
            pltpu.VMEM((16, LANES), F32),
            pltpu.VMEM((tiles, 32, LANES), F32),
            pltpu.VMEM((tiles, 4 * 136, LANES), F32),
        ],
        [prognostic, above, below, far_above, far_below, west, east, cell_offsets, params],
        "track", 40 * 10**6,
    )
    return call(
        advect_kernel,
        [shape(prognostic.shape, BF16)],
        [
            pltpu.VMEM((8 * (rows + 2 * HL), cols + LANES), BF16),
            pltpu.VMEM((144, 256), BF16),
            pltpu.VMEM((16, LANES), F32),
            pltpu.VMEM((tiles, 160, LANES), F32),
            pltpu.VMEM((tiles, 136, LANES), F32),
        ],
        [own, relayed_above, relayed_below, west, east, far_above, far_below, cell_offsets, row_frac, col_frac],
        "advect", 40 * 10**6,
    )[0]


def solution(mesh):
    in_specs = (P(None, None, "lat", "lon"), P(None, "lat", "lon"), P(None, None, "lat", "lon"))
    out_specs = P(None, None, "lat", "lon")
    return jax.shard_map(
        on_device, mesh=mesh, in_specs=in_specs, out_specs=out_specs, check_vma=False
    )
```

```python
import math

import jax
import jax.numpy as jnp
from jax import lax
from jax.experimental import pallas as pl
from jax.experimental.pallas import tpu as pltpu
from jax.sharding import PartitionSpec as P

HO = 8
HL = 10
ITERS = 3
WEST = 7
LANES = 128
F32 = jnp.float32
BF16 = jnp.bfloat16

courant = 2.0


def passed_along(value, axis, by):
    devices = lax.axis_size(axis)
    pairs = [(i, i + by) for i in range(devices) if 0 <= i + by < devices]
    return lax.ppermute(value, axis, pairs)


def from_behind(value, axis, steps):
    count = lax.axis_size(axis)
    pairs = [(source, (source + steps) % count) for source in range(count)]
    return lax.ppermute(value, axis, pairs)


def iota(shape, dim):
    return lax.broadcasted_iota(jnp.int32, shape, dim)


def cubic_weights(t):
    near = (1.5 * t - 2.5) * t * t + 1.0
    s = 1.0 - t
    first = -0.5 * t * s * s
    last = -0.5 * s * t * t
    third = (1.5 * s - 2.5) * s * s + 1.0
    return first, near, third, last


def edge_kernel(fields_ref, edge_west_ref, edge_east_ref, stage):
    channels, levels, rows, cols = fields_ref.shape
    stage[pl.ds(7, rows, stride=8), :] = jnp.zeros((rows, LANES), F32)
    group = iota((8, LANES), 1) // 8
    lane = iota((rows, LANES), 1)

    def pack_level(k, carry):
        for c in range(channels):
            first = pltpu.roll(fields_ref[c, k, :, :LANES].astype(F32), WEST, 1)
            last = pltpu.roll(fields_ref[c, k, :, cols - LANES :].astype(F32), WEST, 1)
            stage[pl.ds(c, rows, stride=8), :] = jnp.where(lane < WEST, last, first)
        west = jnp.zeros((8, LANES), F32)
        east = jnp.zeros((8, LANES), F32)
        for r in range(rows):
            row = stage[8 * r : 8 * r + 8, :]
            slot = rows - 1 - r
            east = jnp.where(group == slot, pltpu.roll(row, 8 * slot, 1), east)
            west = jnp.where(group == slot, pltpu.roll(row, (8 * slot - WEST) % LANES, 1), west)
        edge_west_ref[k] = west.astype(BF16)
        edge_east_ref[k] = east.astype(BF16)
        return carry

    lax.fori_loop(0, levels, pack_level, 0)


def pack_kernel(fields_ref, own_ref, down_ref, up_ref, stage):
    channels, levels, rows, cols = fields_ref.shape
    for t in range(cols // LANES):
        stage[t, pl.ds(7, rows, stride=8), :] = jnp.zeros((rows, LANES), F32)

    def pack_level(k, carry):
        for c in range(channels):
            turned = pltpu.roll(fields_ref[c, k].astype(F32), WEST, 1)
            for t in range(cols // LANES):
                stage[t, pl.ds(c, rows, stride=8), :] = turned[:, LANES * t : LANES * (t + 1)]
        for t in range(cols // LANES):
            cc = slice(LANES * t, LANES * (t + 1))
            own_ref[k, :, cc] = stage[t].astype(BF16)
            down_ref[k, :, cc] = stage[t, (rows - HL) * 8 :, :].astype(BF16)
            up_ref[k, :, cc] = stage[t, : HL * 8, :].astype(BF16)
        return carry

    lax.fori_loop(0, levels, pack_level, 0)


def fill_band_tables(mask, lane_pos):
    offset = iota(mask.shape, 0) - (iota(mask.shape, 1) & (LANES - 1))
    mask[...] = jnp.where((offset >= 0) & (offset < 16), 1.0, 0.0).astype(BF16)
    lane_pos[...] = ((iota(lane_pos.shape, 0) - iota(lane_pos.shape, 1)) & 15).astype(F32)


def band_matrix(compact, mask):
    tiles = [compact * mask[16 * t : 16 * t + 16, :] for t in range(9)]
    tiles.append(jnp.zeros((112, 256), BF16))
    return jnp.concatenate(tiles, axis=0)


def track_kernel(
    wind_ref, above_ref, below_ref, west_ref, east_ref, cells_ref, param_ref,
    row_frac_ref, col_frac_ref,
    stage, spread, mask, lane_pos, dense, taps,
):
    _, levels, rows, cols = wind_ref.shape
    fill_band_tables(mask, lane_pos)

    def edge(west, east, c, first, count):
        def tall(packed, shift):
            parts = []
            for h in range(2):
                part = jnp.broadcast_to(packed[c : c + 1, :].astype(F32), (8, LANES))
                part = pltpu.roll(part, shift + 64 * h, 1)
                parts.append(pltpu.roll(part, 0, 1, stride=8, stride_axis=0))
            return jnp.concatenate(parts, axis=0)

        lane = iota((16, LANES), 1)
        return jnp.where(lane < WEST, tall(west, 8), tall(east, 8 + WEST))[first : first + count]

    def track_level(k, carry):
        lane = iota((32, LANES), 1)
        for c in range(2):
            above = above_ref[k, 8 * c : 8 * c + 8, :].astype(F32)
            below = below_ref[k, 8 * c : 8 * c + 8, :].astype(F32)
            own = wind_ref[c, k].astype(F32)
            turned = pltpu.roll(jnp.concatenate([above, own, below], axis=0), WEST, 1)
            halo = jnp.concatenate(
                [
                    edge(above_ref[k, 16:24, :LANES], above_ref[k, 16:24, LANES : 2 * LANES], c, 8, 8),
                    edge(west_ref[k], east_ref[k], c, 0, 16),
                    edge(below_ref[k, 16:24, :LANES], below_ref[k, 16:24, LANES : 2 * LANES], c, 0, 8),
                ],
                axis=0,
            )
            first = turned[:, :LANES]
            extended = jnp.concatenate(
                [
                    jnp.where(lane < WEST, halo, first),
                    turned[:, LANES:],
                    jnp.where(lane < WEST, first, jnp.where(lane < 15, halo, 0.0)),
                ],
                axis=1,
            )
            for b in range(4):
                moved = extended if b == 0 else pltpu.roll(extended, cols + LANES - b, 1)
                for t in range(cols // LANES + 1):
                    stage[t, pl.ds(2 * b + c, 32, stride=8), :] = moved[:, LANES * t : LANES * (t + 1)]
        for t in range(cols // LANES + 1):
            spread[:, LANES * t : LANES * (t + 1)] = stage[t].astype(BF16)

        row_off = cells_ref[0, k]
        col_off = cells_ref[1, k]
        row_mid = row_off >> 1
        col_mid = col_off >> 1
        for t in range(cols // LANES):
            dense[t, 0:16, :] = (col_mid[:, LANES * t : LANES * (t + 1)] + 6).astype(F32)
            dense[t, 16:32, :] = (row_mid[:, LANES * t : LANES * (t + 1)] + 4).astype(F32)

        def gather(pair, carry):
            y = 2 * pair
            start = pl.multiple_of(16 * pair + 16, 16)
            for block in range(cols // LANES):
                lo = block * LANES
                halves = []
                for n in range(2):
                    at = dense[block, pl.ds(y + n, 8, stride=0), :]
                    at = jnp.concatenate([at, at], axis=0)
                    halves.append(jnp.where(lane_pos[...] == at, 1.0, 0.0))
                compact = jnp.concatenate(halves, axis=1).astype(BF16)
                found = jnp.dot(
                    spread[pl.ds(start, 112), lo : lo + 256],
                    band_matrix(compact, mask),
                    preferred_element_type=F32,
                )
                for n in range(2):
                    depth = dense[block, pl.ds(16 + y + n, 8, stride=0), :]
                    v = [
                        found[8 * (1 + n + i) : 8 * (2 + n + i), n * LANES : (n + 1) * LANES]
                        for i in range(12)
                    ]
                    whole = depth >= 8.0
                    v = [jnp.where(whole, v[i + 8], v[i]) for i in range(4)] + v[4:]
                    depth = jnp.where(whole, depth - 8.0, depth)
                    for step, count in ((4, 7), (2, 5), (1, 4)):
                        far = depth >= float(step)
                        v = [jnp.where(far, v[i + step], v[i]) for i in range(count)]
                        depth = jnp.where(far, depth - float(step), depth)
                    for a in range(4):
                        taps[block, pl.ds(a * 136 + y + n, 8, stride=17), :] = v[a]
            return carry

        lax.fori_loop(0, rows // 2, gather, 0, unroll=True)

        for half in range(rows // 8):
            for tile in range(cols // LANES):
                rr = slice(8 * half, 8 * half + 8)
                cc = slice(LANES * tile, LANES * tile + LANES)
                cy = param_ref[16:24, :]
                dy = param_ref[24:32, :]
                dx = param_ref[32:40, :]
                cx = param_ref[rr, :]
                oy = row_off[rr, cc]
                ox = col_off[rr, cc]
                y_odd = (oy & 1).astype(F32)
                x_odd = (ox & 1).astype(F32)
                oyf = oy.astype(F32) + 0.5
                oxf = ox.astype(F32) + 0.5
                fy = jnp.full((8, LANES), 0.5, F32)
                fx = fy
                for _ in range(ITERS):
                    wy = cubic_weights((y_odd + fy) * 0.5)
                    wx = [w.astype(BF16).astype(F32) for w in cubic_weights((x_odd + fx) * 0.5)]
                    mid = []
                    for c in range(2):
                        total = None
                        for a in range(4):
                            along = None
                            for b in range(4):
                                base = a * 136 + (2 * b + c) * 17 + 8 * half
                                term = wx[b] * taps[tile, base : base + 8, :]
                                along = term if along is None else along + term
                            along = wy[a] * along
                            total = along if total is None else total + along
                        mid.append(total)
                    lx = dx * jnp.tanh(mid[0] * cx)
                    ly = dy * jnp.tanh(mid[1] * cy)
                    fy = 0.5 + 0.5 * jnp.tanh(0.5 * (ly - oyf))
                    fx = 0.5 + 0.5 * jnp.tanh(0.5 * (lx - oxf))
                row_frac_ref[k, rr, cc] = fy
                col_frac_ref[k, rr, cc] = fx
        return carry

    lax.fori_loop(0, levels, track_level, 0)


def advect_kernel(
    own_ref, above_ref, below_ref, west_ref, east_ref, far_above_ref, far_below_ref, cells_ref,
    row_frac_ref, col_frac_ref,
    out_ref,
    spread, mask, lane_pos, dense, result,
):
    channels, levels, rows, cols = out_ref.shape
    fill_band_tables(mask, lane_pos)

    def place(block, west, east, first, count, at):
        west = west.astype(F32)
        east = east.astype(F32)
        halo = []
        lane = iota((8, LANES), 1)
        for r in range(first, first + count):
            a = pltpu.roll(west, (8 * r + 8) % LANES, 1)
            b = pltpu.roll(east, (8 * r + 8 + WEST) % LANES, 1)
            halo.append(jnp.where(lane < WEST, a, jnp.where(lane < 15, b, 0.0)))
        halo = jnp.concatenate(halo, axis=0)
        lanes = iota((8 * count, LANES), 1)
        start = block[:, :LANES].astype(F32)
        spread[at : at + 8 * count, :LANES] = jnp.where(lanes < WEST, halo, start).astype(BF16)
        spread[at : at + 8 * count, LANES:cols] = block[:, LANES:]
        spread[at : at + 8 * count, cols:] = jnp.where(lanes < WEST, start, halo).astype(BF16)

    def advect_level(k, carry):
        place(above_ref[k], far_above_ref[k, 16:24, :LANES], far_above_ref[k, 16:24, LANES : 2 * LANES], rows - HL, HL, 0)
        place(own_ref[k], west_ref[k], east_ref[k], 0, rows, 8 * HL)
        place(below_ref[k], far_below_ref[k, 16:24, :LANES], far_below_ref[k, 16:24, LANES : 2 * LANES], 0, HL, 8 * (HL + rows))

        for t in range(cols // LANES):
            cc = slice(LANES * t, LANES * (t + 1))
            dense[t, 0:16, :] = (cells_ref[1, k, :, cc] + 6).astype(F32)
            dense[t, 16:32, :] = (cells_ref[0, k, :, cc] + 8).astype(F32)
            for i, w in enumerate(cubic_weights(col_frac_ref[k, :, cc])):
                dense[t, 32 + 16 * i : 48 + 16 * i, :] = w.astype(BF16).astype(F32)
            for i, w in enumerate(cubic_weights(row_frac_ref[k, :, cc])):
                dense[t, 96 + 16 * i : 112 + 16 * i, :] = w

        def sample(pair, carry):
            y = 2 * pair
            start = pl.multiple_of(16 * pair, 16)
            for block in range(cols // LANES):
                lo = block * LANES
                halves = []
                for n in range(2):
                    def wide(part):
                        return dense[block, pl.ds(16 * part + y + n, 8, stride=0), :]

                    at = wide(0)
                    w = [wide(2 + b) for b in range(4)]
                    both = []
                    for h in range(2):
                        rel = lane_pos[8 * h : 8 * h + 8, :] - at
                        picked = jnp.where(rel == 3.0, w[3], 0.0)
                        picked = jnp.where(rel == 2.0, w[2], picked)
                        picked = jnp.where(rel == 1.0, w[1], picked)
                        both.append(jnp.where(rel == 0.0, w[0], picked))
                    halves.append(jnp.concatenate(both, axis=0))
                compact = jnp.concatenate(halves, axis=1).astype(BF16)
                mixed = jnp.dot(
                    spread[pl.ds(start, 176), lo : lo + 256],
                    band_matrix(compact, mask),
                    preferred_element_type=F32,
                )
                for n in range(2):
                    depth = dense[block, pl.ds(16 + y + n, 8, stride=0), :]
                    v = [
                        mixed[8 * (1 + n + i) : 8 * (2 + n + i), n * LANES : (n + 1) * LANES]
                        for i in range(20)
                    ]
                    whole = depth >= 16.0
                    v = [jnp.where(whole, v[i + 16], v[i]) for i in range(4)] + v[4:]
                    depth = jnp.where(whole, depth - 16.0, depth)
                    for step, count in ((8, 11), (4, 7), (2, 5), (1, 4)):
                        far = depth >= float(step)
                        v = [jnp.where(far, v[i + step], v[i]) for i in range(count)]
                        depth = jnp.where(far, depth - float(step), depth)
                    total = None
                    for a in range(4):
                        weight = dense[block, pl.ds(96 + 16 * a + y + n, 8, stride=0), :]
                        total = weight * v[a] if total is None else total + weight * v[a]
                    result[block, pl.ds(y + n, 8, stride=17), :] = total
            return carry

        lax.fori_loop(0, rows // 2, sample, 0, unroll=True)
        for c in range(channels):
            for t in range(cols // LANES):
                cc = slice(LANES * t, LANES * (t + 1))
                out_ref[c, k, :, cc] = result[t, 17 * c : 17 * c + 16, :].astype(BF16)
        return carry

    lax.fori_loop(0, levels, advect_level, 0)


def call(kernel, outs, scratch, args, name, flops):
    moved = sum(a.size * a.dtype.itemsize for a in list(args) + list(outs))
    in_vmem = pl.BlockSpec(memory_space=pltpu.VMEM)
    return pl.pallas_call(
        kernel,
        in_specs=[in_vmem] * len(args),
        out_specs=[in_vmem] * len(outs),
        out_shape=outs,
        scratch_shapes=scratch,
        cost_estimate=pl.CostEstimate(flops=flops, bytes_accessed=moved, transcendentals=0),
        compiler_params=pltpu.CompilerParams(vmem_limit_bytes=24 << 20),
        name=name,
    )(*args)


def on_device(prognostic, halo_depth, cell_offsets):
    channels, levels, rows, cols = prognostic.shape
    tiles = cols // LANES
    shape = jax.ShapeDtypeStruct
    edge = shape((levels, 8, LANES), BF16)
    edge_west, edge_east = call(
        edge_kernel, [edge, edge], [pltpu.VMEM((8 * rows, LANES), F32)], [prognostic], "edge", 10**6
    )
    west = from_behind(edge_east, "lon", 1)
    east = from_behind(edge_west, "lon", -1)
    own, down, up = call(
        pack_kernel,
        [shape((levels, 8 * n, cols), BF16) for n in (rows, HL, HL)],
        [pltpu.VMEM((tiles, 8 * rows, LANES), F32)],
        [prognostic], "pack", 10**6,
    )

    lat_total = rows * lax.axis_size("lat")
    lat_index = (lax.axis_index("lat") * rows + jnp.arange(rows, dtype=jnp.int32)).astype(F32)
    coslat = jnp.cos((lat_index + 0.5) * (math.pi / lat_total) - 0.5 * math.pi)
    reach = halo_depth[:, 0, 0].astype(F32) - 1.0
    params = jnp.concatenate(
        [-courant / (coslat * reach[1]), jnp.repeat(jnp.stack([-courant / reach[0], reach[0], reach[1]]), 8)]
    )
    params = jnp.broadcast_to(params[:, None], (rows + 24, LANES))

    edges = jnp.concatenate([west, east, jnp.zeros((levels, 8, cols - 2 * LANES), BF16)], axis=2)
    send_down = jnp.concatenate([prognostic[0, :, rows - 8 :], prognostic[1, :, rows - 8 :], edges], axis=1)
    send_up = jnp.concatenate([prognostic[0, :, :8], prognostic[1, :, :8], edges], axis=1)
    send_down, send_up, params = lax.optimization_barrier((send_down, send_up, params))
    far_above = passed_along(send_down, "lat", 1)
    far_below = passed_along(send_up, "lat", -1)
    above = passed_along(down, "lat", 1)
    below = passed_along(up, "lat", -1)

    frac = shape((levels, rows, cols), F32)
    row_frac, col_frac = call(
        track_kernel,
        [frac, frac],
        [
            pltpu.VMEM((tiles + 1, 8 * 32, LANES), F32),
            pltpu.VMEM((8 * 32, cols + LANES), BF16),
            pltpu.VMEM((144, 256), BF16),
            pltpu.VMEM((16, LANES), F32),
            pltpu.VMEM((tiles, 32, LANES), F32),
            pltpu.VMEM((tiles, 4 * 136, LANES), F32),
        ],
        [prognostic, far_above, far_below, west, east, cell_offsets, params],
        "track", 10**10,
    )
    return call(
        advect_kernel,
        [shape(prognostic.shape, BF16)],
        [
            pltpu.VMEM((8 * (rows + 2 * HL), cols + LANES), BF16),
            pltpu.VMEM((144, 256), BF16),
            pltpu.VMEM((16, LANES), F32),
            pltpu.VMEM((tiles, 160, LANES), F32),
            pltpu.VMEM((tiles, 136, LANES), F32),
        ],
        [own, above, below, west, east, far_above, far_below, cell_offsets, row_frac, col_frac],
        "advect", 40 * 10**6,
    )[0]


def solution(mesh):
    in_specs = (P(None, None, "lat", "lon"), P(None, "lat", "lon"), P(None, None, "lat", "lon"))
    out_specs = P(None, None, "lat", "lon")
    return jax.shard_map(
        on_device, mesh=mesh, in_specs=in_specs, out_specs=out_specs, check_vma=False
    )
```

```python
import math

import jax
import jax.numpy as jnp
from jax import lax
from jax.experimental import pallas as pl
from jax.experimental.pallas import tpu as pltpu
from jax.sharding import PartitionSpec as P

HO = 8
HL = 10
ITERS = 3
WEST = 7
LANES = 128
SLOTS = 4
F32 = jnp.float32
BF16 = jnp.bfloat16

courant = 2.0


def passed_along(value, axis, by):
    devices = lax.axis_size(axis)
    pairs = [(i, i + by) for i in range(devices) if 0 <= i + by < devices]
    return lax.ppermute(value, axis, pairs)


def from_behind(value, axis, steps):
    count = lax.axis_size(axis)
    pairs = [(source, (source + steps) % count) for source in range(count)]
    return lax.ppermute(value, axis, pairs)


def iota(shape, dim):
    return lax.broadcasted_iota(jnp.int32, shape, dim)


def cubic_weights(t):
    near = (1.5 * t - 2.5) * t * t + 1.0
    s = 1.0 - t
    first = -0.5 * t * s * s
    last = -0.5 * s * t * t
    third = (1.5 * s - 2.5) * s * s + 1.0
    return first, near, third, last


def edge_kernel(fields_ref, edge_west_ref, edge_east_ref, stage):
    channels, levels, rows, cols = fields_ref.shape
    stage[pl.ds(7, rows, stride=8), :] = jnp.zeros((rows, LANES), F32)
    group = iota((8, LANES), 1) // 8
    lane = iota((rows, LANES), 1)

    def pack_level(k, carry):
        for c in range(channels):
            first = pltpu.roll(fields_ref[c, k, :, :LANES].astype(F32), WEST, 1)
            last = pltpu.roll(fields_ref[c, k, :, cols - LANES :].astype(F32), WEST, 1)
            stage[pl.ds(c, rows, stride=8), :] = jnp.where(lane < WEST, last, first)
        west = jnp.zeros((8, LANES), F32)
        east = jnp.zeros((8, LANES), F32)
        for r in range(rows):
            row = stage[8 * r : 8 * r + 8, :]
            slot = rows - 1 - r
            east = jnp.where(group == slot, pltpu.roll(row, 8 * slot, 1), east)
            west = jnp.where(group == slot, pltpu.roll(row, (8 * slot - WEST) % LANES, 1), west)
        edge_west_ref[k] = west.astype(BF16)
        edge_east_ref[k] = east.astype(BF16)
        return carry

    lax.fori_loop(0, levels, pack_level, 0)


def pack_kernel(fields_ref, own_ref, down_ref, up_ref, stage):
    channels, levels, rows, cols = fields_ref.shape
    for t in range(cols // LANES):
        stage[t, pl.ds(7, rows, stride=8), :] = jnp.zeros((rows, LANES), F32)

    def pack_level(k, carry):
        for c in range(channels):
            turned = pltpu.roll(fields_ref[c, k].astype(F32), WEST, 1)
            for t in range(cols // LANES):
                stage[t, pl.ds(c, rows, stride=8), :] = turned[:, LANES * t : LANES * (t + 1)]
        for t in range(cols // LANES):
            cc = slice(LANES * t, LANES * (t + 1))
            own_ref[k, :, cc] = stage[t].astype(BF16)
            down_ref[k, :, cc] = stage[t, (rows - HL) * 8 :, :].astype(BF16)
            up_ref[k, :, cc] = stage[t, : HL * 8, :].astype(BF16)
        return carry

    lax.fori_loop(0, levels, pack_level, 0)


def fill_band_tables(mask, lane_pos):
    offset = iota(mask.shape, 0) - (iota(mask.shape, 1) & (LANES - 1))
    mask[...] = jnp.where((offset >= 0) & (offset < 16), 1.0, 0.0).astype(BF16)
    lane_pos[...] = ((iota(lane_pos.shape, 0) - iota(lane_pos.shape, 1)) & 15).astype(F32)


def band_matrix(compact, mask):
    tiles = [compact * mask[16 * t : 16 * t + 16, :] for t in range(9)]
    tiles.append(jnp.zeros((112, 256), BF16))
    return jnp.concatenate(tiles, axis=0)


def track_kernel(
    wind_ref, above_ref, below_ref, west_ref, east_ref, cells_ref, param_ref,
    row_frac_ref, col_frac_ref,
    stages, spreads, mask, lane_pos, denses, tapss,
):
    _, levels, rows, cols = wind_ref.shape
    fill_band_tables(mask, lane_pos)

    def edge(west, east, c, first, count):
        def tall(packed, shift):
            parts = []
            for h in range(2):
                part = jnp.broadcast_to(packed[c : c + 1, :].astype(F32), (8, LANES))
                part = pltpu.roll(part, shift + 64 * h, 1)
                parts.append(pltpu.roll(part, 0, 1, stride=8, stride_axis=0))
            return jnp.concatenate(parts, axis=0)

        lane = iota((16, LANES), 1)
        return jnp.where(lane < WEST, tall(west, 8), tall(east, 8 + WEST))[first : first + count]

    def prepare(k, slot):
        stage = stages.at[slot]
        spread = spreads.at[slot]
        dense = denses.at[slot]
        lane = iota((32, LANES), 1)
        for c in range(2):
            above = above_ref[k, 8 * c : 8 * c + 8, :].astype(F32)
            below = below_ref[k, 8 * c : 8 * c + 8, :].astype(F32)
            own = wind_ref[c, k].astype(F32)
            turned = pltpu.roll(jnp.concatenate([above, own, below], axis=0), WEST, 1)
            halo = jnp.concatenate(
                [
                    edge(above_ref[k, 16:24, :LANES], above_ref[k, 16:24, LANES : 2 * LANES], c, 8, 8),
                    edge(west_ref[k], east_ref[k], c, 0, 16),
                    edge(below_ref[k, 16:24, :LANES], below_ref[k, 16:24, LANES : 2 * LANES], c, 0, 8),
                ],
                axis=0,
            )
            first = turned[:, :LANES]
            extended = jnp.concatenate(
                [
                    jnp.where(lane < WEST, halo, first),
                    turned[:, LANES:],
                    jnp.where(lane < WEST, first, jnp.where(lane < 15, halo, 0.0)),
                ],
                axis=1,
            )
            for b in range(4):
                moved = extended if b == 0 else pltpu.roll(extended, cols + LANES - b, 1)
                for t in range(cols // LANES + 1):
                    stage[t, pl.ds(2 * b + c, 32, stride=8), :] = moved[:, LANES * t : LANES * (t + 1)]
        for t in range(cols // LANES + 1):
            spread[:, LANES * t : LANES * (t + 1)] = stage[t].astype(BF16)

        row_off = cells_ref[0, k]
        col_off = cells_ref[1, k]
        row_mid = row_off >> 1
        col_mid = col_off >> 1
        for t in range(cols // LANES):
            dense[t, 0:16, :] = (col_mid[:, LANES * t : LANES * (t + 1)] + 6).astype(F32)
            dense[t, 16:32, :] = (row_mid[:, LANES * t : LANES * (t + 1)] + 4).astype(F32)

    def collect(slot):
        spread = spreads.at[slot]
        dense = denses.at[slot]
        taps = tapss.at[slot]
        def gather(pair, carry):
            y = 2 * pair
            start = pl.multiple_of(16 * pair + 16, 16)
            for block in range(cols // LANES):
                lo = block * LANES
                halves = []
                for n in range(2):
                    at = dense[block, pl.ds(y + n, 8, stride=0), :]
                    at = jnp.concatenate([at, at], axis=0)
                    halves.append(jnp.where(lane_pos[...] == at, 1.0, 0.0))
                compact = jnp.concatenate(halves, axis=1).astype(BF16)
                found = jnp.dot(
                    spread[pl.ds(start, 112), lo : lo + 256],
                    band_matrix(compact, mask),
                    preferred_element_type=F32,
                )
                for n in range(2):
                    depth = dense[block, pl.ds(16 + y + n, 8, stride=0), :]
                    v = [
                        found[8 * (1 + n + i) : 8 * (2 + n + i), n * LANES : (n + 1) * LANES]
                        for i in range(12)
                    ]
                    whole = depth >= 8.0
                    v = [jnp.where(whole, v[i + 8], v[i]) for i in range(4)] + v[4:]
                    depth = jnp.where(whole, depth - 8.0, depth)
                    for step, count in ((4, 7), (2, 5), (1, 4)):
                        far = depth >= float(step)
                        v = [jnp.where(far, v[i + step], v[i]) for i in range(count)]
                        depth = jnp.where(far, depth - float(step), depth)
                    for a in range(4):
                        taps[block, pl.ds(a * 136 + y + n, 8, stride=17), :] = v[a]
            return carry

        for pair in range(rows // 2):
            gather(pair, 0)

    def iterate(k, slot):
        taps = tapss.at[slot]
        row_off = cells_ref[0, k]
        col_off = cells_ref[1, k]
        for half in range(rows // 8):
            for tile in range(cols // LANES):
                rr = slice(8 * half, 8 * half + 8)
                cc = slice(LANES * tile, LANES * tile + LANES)
                cy = param_ref[16:24, :]
                dy = param_ref[24:32, :]
                dx = param_ref[32:40, :]
                cx = param_ref[rr, :]
                oy = row_off[rr, cc]
                ox = col_off[rr, cc]
                y_odd = (oy & 1).astype(F32)
                x_odd = (ox & 1).astype(F32)
                oyf = oy.astype(F32) + 0.5
                oxf = ox.astype(F32) + 0.5
                fy = jnp.full((8, LANES), 0.5, F32)
                fx = fy
                for _ in range(ITERS):
                    wy = cubic_weights((y_odd + fy) * 0.5)
                    wx = [w.astype(BF16).astype(F32) for w in cubic_weights((x_odd + fx) * 0.5)]
                    mid = []
                    for c in range(2):
                        total = None
                        for a in range(4):
                            along = None
                            for b in range(4):
                                base = a * 136 + (2 * b + c) * 17 + 8 * half
                                term = wx[b] * taps[tile, base : base + 8, :]
                                along = term if along is None else along + term
                            along = wy[a] * along
                            total = along if total is None else total + along
                        mid.append(total)
                    lx = dx * jnp.tanh(mid[0] * cx)
                    ly = dy * jnp.tanh(mid[1] * cy)
                    fy = 0.5 + 0.5 * jnp.tanh(0.5 * (ly - oyf))
                    fx = 0.5 + 0.5 * jnp.tanh(0.5 * (lx - oxf))
                row_frac_ref[k, rr, cc] = fy
                col_frac_ref[k, rr, cc] = fx

    def track_levels(group, carry):
        for slot in range(SLOTS):
            prepare(SLOTS * group + slot, slot)
        for slot in range(SLOTS):
            collect(slot)
            iterate(SLOTS * group + slot, slot)
        return carry

    lax.fori_loop(0, levels // SLOTS, track_levels, 0)


def advect_kernel(
    own_ref, above_ref, below_ref, west_ref, east_ref, far_above_ref, far_below_ref, cells_ref,
    row_frac_ref, col_frac_ref,
    out_ref,
    spreads, mask, lane_pos, denses, results,
):
    channels, levels, rows, cols = out_ref.shape
    fill_band_tables(mask, lane_pos)

    def place(spread, block, west, east, first, count, at):
        west = west.astype(F32)
        east = east.astype(F32)
        halo = []
        lane = iota((8, LANES), 1)
        for r in range(first, first + count):
            a = pltpu.roll(west, (8 * r + 8) % LANES, 1)
            b = pltpu.roll(east, (8 * r + 8 + WEST) % LANES, 1)
            halo.append(jnp.where(lane < WEST, a, jnp.where(lane < 15, b, 0.0)))
        halo = jnp.concatenate(halo, axis=0)
        lanes = iota((8 * count, LANES), 1)
        start = block[:, :LANES].astype(F32)
        spread[at : at + 8 * count, :LANES] = jnp.where(lanes < WEST, halo, start).astype(BF16)
        spread[at : at + 8 * count, LANES:cols] = block[:, LANES:]
        spread[at : at + 8 * count, cols:] = jnp.where(lanes < WEST, start, halo).astype(BF16)

    def prepare(k, slot):
        spread = spreads.at[slot]
        dense = denses.at[slot]
        place(spread, above_ref[k], far_above_ref[k, 16:24, :LANES], far_above_ref[k, 16:24, LANES : 2 * LANES], rows - HL, HL, 0)
        place(spread, own_ref[k], west_ref[k], east_ref[k], 0, rows, 8 * HL)
        place(spread, below_ref[k], far_below_ref[k, 16:24, :LANES], far_below_ref[k, 16:24, LANES : 2 * LANES], 0, HL, 8 * (HL + rows))

        for t in range(cols // LANES):
            cc = slice(LANES * t, LANES * (t + 1))
            dense[t, 0:16, :] = (cells_ref[1, k, :, cc] + 6).astype(F32)
            dense[t, 16:32, :] = (cells_ref[0, k, :, cc] + 8).astype(F32)
            for i, w in enumerate(cubic_weights(col_frac_ref[k, :, cc])):
                dense[t, 32 + 16 * i : 48 + 16 * i, :] = w.astype(BF16).astype(F32)
            for i, w in enumerate(cubic_weights(row_frac_ref[k, :, cc])):
                dense[t, 96 + 16 * i : 112 + 16 * i, :] = w

    def collect(k, slot):
        spread = spreads.at[slot]
        dense = denses.at[slot]
        result = results.at[slot]
        def sample(pair, carry):
            y = 2 * pair
            start = pl.multiple_of(16 * pair, 16)
            for block in range(cols // LANES):
                lo = block * LANES
                halves = []
                for n in range(2):
                    def wide(part):
                        return dense[block, pl.ds(16 * part + y + n, 8, stride=0), :]

                    at = wide(0)
                    w = [wide(2 + b) for b in range(4)]
                    both = []
                    for h in range(2):
                        rel = lane_pos[8 * h : 8 * h + 8, :] - at
                        picked = jnp.where(rel == 3.0, w[3], 0.0)
                        picked = jnp.where(rel == 2.0, w[2], picked)
                        picked = jnp.where(rel == 1.0, w[1], picked)
                        both.append(jnp.where(rel == 0.0, w[0], picked))
                    halves.append(jnp.concatenate(both, axis=0))
                compact = jnp.concatenate(halves, axis=1).astype(BF16)
                mixed = jnp.dot(
                    spread[pl.ds(start, 176), lo : lo + 256],
                    band_matrix(compact, mask),
                    preferred_element_type=F32,
                )
                for n in range(2):
                    depth = dense[block, pl.ds(16 + y + n, 8, stride=0), :]
                    v = [
                        mixed[8 * (1 + n + i) : 8 * (2 + n + i), n * LANES : (n + 1) * LANES]
                        for i in range(20)
                    ]
                    whole = depth >= 16.0
                    v = [jnp.where(whole, v[i + 16], v[i]) for i in range(4)] + v[4:]
                    depth = jnp.where(whole, depth - 16.0, depth)
                    for step, count in ((8, 11), (4, 7), (2, 5), (1, 4)):
                        far = depth >= float(step)
                        v = [jnp.where(far, v[i + step], v[i]) for i in range(count)]
                        depth = jnp.where(far, depth - float(step), depth)
                    total = None
                    for a in range(4):
                        weight = dense[block, pl.ds(96 + 16 * a + y + n, 8, stride=0), :]
                        total = weight * v[a] if total is None else total + weight * v[a]
                    result[block, pl.ds(y + n, 8, stride=17), :] = total
            return carry

        for pair in range(rows // 2):
            sample(pair, 0)
        for c in range(channels):
            for t in range(cols // LANES):
                cc = slice(LANES * t, LANES * (t + 1))
                out_ref[c, k, :, cc] = result[t, 17 * c : 17 * c + 16, :].astype(BF16)

    def advect_levels(group, carry):
        for slot in range(SLOTS):
            prepare(SLOTS * group + slot, slot)
        for slot in range(SLOTS):
            collect(SLOTS * group + slot, slot)
        return carry

    lax.fori_loop(0, levels // SLOTS, advect_levels, 0)


def call(kernel, outs, scratch, args, name, flops):
    moved = sum(a.size * a.dtype.itemsize for a in list(args) + list(outs))
    in_vmem = pl.BlockSpec(memory_space=pltpu.VMEM)
    return pl.pallas_call(
        kernel,
        in_specs=[in_vmem] * len(args),
        out_specs=[in_vmem] * len(outs),
        out_shape=outs,
        scratch_shapes=scratch,
        cost_estimate=pl.CostEstimate(flops=flops, bytes_accessed=moved, transcendentals=0),
        compiler_params=pltpu.CompilerParams(vmem_limit_bytes=24 << 20),
        name=name,
    )(*args)


def on_device(prognostic, halo_depth, cell_offsets):
    channels, levels, rows, cols = prognostic.shape
    tiles = cols // LANES
    shape = jax.ShapeDtypeStruct
    edge = shape((levels, 8, LANES), BF16)
    edge_west, edge_east = call(
        edge_kernel, [edge, edge], [pltpu.VMEM((8 * rows, LANES), F32)], [prognostic], "edge", 10**6
    )
    west = from_behind(edge_east, "lon", 1)
    east = from_behind(edge_west, "lon", -1)
    own, down, up = call(
        pack_kernel,
        [shape((levels, 8 * n, cols), BF16) for n in (rows, HL, HL)],
        [pltpu.VMEM((tiles, 8 * rows, LANES), F32)],
        [prognostic], "pack", 10**6,
    )

    lat_total = rows * lax.axis_size("lat")
    lat_index = (lax.axis_index("lat") * rows + jnp.arange(rows, dtype=jnp.int32)).astype(F32)
    coslat = jnp.cos((lat_index + 0.5) * (math.pi / lat_total) - 0.5 * math.pi)
    reach = halo_depth[:, 0, 0].astype(F32) - 1.0
    params = jnp.concatenate(
        [-courant / (coslat * reach[1]), jnp.repeat(jnp.stack([-courant / reach[0], reach[0], reach[1]]), 8)]
    )
    params = jnp.broadcast_to(params[:, None], (rows + 24, LANES))

    edges = jnp.concatenate([west, east, jnp.zeros((levels, 8, cols - 2 * LANES), BF16)], axis=2)
    send_down = jnp.concatenate([prognostic[0, :, rows - 8 :], prognostic[1, :, rows - 8 :], edges], axis=1)
    send_up = jnp.concatenate([prognostic[0, :, :8], prognostic[1, :, :8], edges], axis=1)
    send_down, send_up, params = lax.optimization_barrier((send_down, send_up, params))
    far_above = passed_along(send_down, "lat", 1)
    far_below = passed_along(send_up, "lat", -1)
    above = passed_along(down, "lat", 1)
    below = passed_along(up, "lat", -1)

    frac = shape((levels, rows, cols), F32)
    row_frac, col_frac = call(
        track_kernel,
        [frac, frac],
        [
            pltpu.VMEM((SLOTS, tiles + 1, 8 * 32, LANES), F32),
            pltpu.VMEM((SLOTS, 8 * 32, cols + LANES), BF16),
            pltpu.VMEM((144, 256), BF16),
            pltpu.VMEM((16, LANES), F32),
            pltpu.VMEM((SLOTS, tiles, 32, LANES), F32),
            pltpu.VMEM((SLOTS, tiles, 4 * 136, LANES), F32),
        ],
        [prognostic, far_above, far_below, west, east, cell_offsets, params],
        "track", 10**10,
    )
    return call(
        advect_kernel,
        [shape(prognostic.shape, BF16)],
        [
            pltpu.VMEM((SLOTS, 8 * (rows + 2 * HL), cols + LANES), BF16),
            pltpu.VMEM((144, 256), BF16),
            pltpu.VMEM((16, LANES), F32),
            pltpu.VMEM((SLOTS, tiles, 160, LANES), F32),
            pltpu.VMEM((SLOTS, tiles, 136, LANES), F32),
        ],
        [own, above, below, west, east, far_above, far_below, cell_offsets, row_frac, col_frac],
        "advect", 40 * 10**6,
    )[0]


def solution(mesh):
    in_specs = (P(None, None, "lat", "lon"), P(None, "lat", "lon"), P(None, None, "lat", "lon"))
    out_specs = P(None, None, "lat", "lon")
    return jax.shard_map(
        on_device, mesh=mesh, in_specs=in_specs, out_specs=out_specs, check_vma=False
    )
```

```python
import math

import jax
import jax.numpy as jnp
from jax import lax
from jax.experimental import pallas as pl
from jax.experimental.pallas import tpu as pltpu
from jax.sharding import PartitionSpec as P

HO = 8
HL = 10
ITERS = 3
WEST = 7
LANES = 128
SLOTS = 4
F32 = jnp.float32
BF16 = jnp.bfloat16

courant = 2.0


def passed_along(value, axis, by):
    devices = lax.axis_size(axis)
    pairs = [(i, i + by) for i in range(devices) if 0 <= i + by < devices]
    return lax.ppermute(value, axis, pairs)


def from_behind(value, axis, steps):
    count = lax.axis_size(axis)
    pairs = [(source, (source + steps) % count) for source in range(count)]
    return lax.ppermute(value, axis, pairs)


def iota(shape, dim):
    return lax.broadcasted_iota(jnp.int32, shape, dim)


def cubic_weights(t):
    near = (1.5 * t - 2.5) * t * t + 1.0
    s = 1.0 - t
    first = -0.5 * t * s * s
    last = -0.5 * s * t * t
    third = (1.5 * s - 2.5) * s * s + 1.0
    return first, near, third, last


def edge_kernel(fields_ref, edge_west_ref, edge_east_ref, stage):
    channels, levels, rows, cols = fields_ref.shape
    stage[pl.ds(7, rows, stride=8), :] = jnp.zeros((rows, LANES), F32)
    group = iota((8, LANES), 1) // 8
    lane = iota((rows, LANES), 1)

    def pack_level(k, carry):
        for c in range(channels):
            first = pltpu.roll(fields_ref[c, k, :, :LANES].astype(F32), WEST, 1)
            last = pltpu.roll(fields_ref[c, k, :, cols - LANES :].astype(F32), WEST, 1)
            stage[pl.ds(c, rows, stride=8), :] = jnp.where(lane < WEST, last, first)
        west = jnp.zeros((8, LANES), F32)
        east = jnp.zeros((8, LANES), F32)
        for r in range(rows):
            row = stage[8 * r : 8 * r + 8, :]
            slot = rows - 1 - r
            east = jnp.where(group == slot, pltpu.roll(row, 8 * slot, 1), east)
            west = jnp.where(group == slot, pltpu.roll(row, (8 * slot - WEST) % LANES, 1), west)
        edge_west_ref[k] = west.astype(BF16)
        edge_east_ref[k] = east.astype(BF16)
        return carry

    lax.fori_loop(0, levels, pack_level, 0)


def pack_kernel(fields_ref, own_ref, down_ref, up_ref, stage):
    channels, levels, rows, cols = fields_ref.shape
    for t in range(cols // LANES):
        stage[t, pl.ds(7, rows, stride=8), :] = jnp.zeros((rows, LANES), F32)

    def pack_level(k, carry):
        for c in range(channels):
            turned = pltpu.roll(fields_ref[c, k].astype(F32), WEST, 1)
            for t in range(cols // LANES):
                stage[t, pl.ds(c, rows, stride=8), :] = turned[:, LANES * t : LANES * (t + 1)]
        for t in range(cols // LANES):
            cc = slice(LANES * t, LANES * (t + 1))
            own_ref[k, :, cc] = stage[t].astype(BF16)
            down_ref[k, :, cc] = stage[t, (rows - HL) * 8 :, :].astype(BF16)
            up_ref[k, :, cc] = stage[t, : HL * 8, :].astype(BF16)
        return carry

    lax.fori_loop(0, levels, pack_level, 0)


def fill_band_tables(mask, lane_pos):
    offset = iota(mask.shape, 0) - (iota(mask.shape, 1) & (LANES - 1))
    mask[...] = jnp.where((offset >= 0) & (offset < 16), 1.0, 0.0).astype(BF16)
    lane_pos[...] = ((iota(lane_pos.shape, 0) - iota(lane_pos.shape, 1)) & 15).astype(F32)


def band_matrix(compact, mask):
    tiles = [compact * mask[16 * t : 16 * t + 16, :] for t in range(9)]
    tiles.append(jnp.zeros((112, 256), BF16))
    return jnp.concatenate(tiles, axis=0)


def track_kernel(
    wind_ref, above_ref, below_ref, west_ref, east_ref, cells_ref, depth_ref,
    row_frac_ref, col_frac_ref,
    stages, spreads, mask, lane_pos, denses, tapss, param_ref,
):
    _, levels, rows, cols = wind_ref.shape
    fill_band_tables(mask, lane_pos)
    lat_total = rows * lax.axis_size("lat")
    lat_index = (lax.axis_index("lat") * rows + iota((rows, LANES), 0)).astype(F32)
    coslat = jnp.cos((lat_index + 0.5) * (math.pi / lat_total) - 0.5 * math.pi)
    reach_y = jnp.full((8, LANES), depth_ref[0, 0, 0], jnp.int32).astype(F32) - 1.0
    reach_x = jnp.full((8, LANES), depth_ref[1, 0, 0], jnp.int32).astype(F32) - 1.0
    for half in range(rows // 8):
        part = slice(8 * half, 8 * half + 8)
        param_ref[part, :] = -courant / (coslat[part, :] * reach_x)
    param_ref[16:24, :] = -courant / reach_y
    param_ref[24:32, :] = reach_y
    param_ref[32:40, :] = reach_x

    def edge(west, east, c, first, count):
        def tall(packed, shift):
            parts = []
            for h in range(2):
                part = jnp.broadcast_to(packed[c : c + 1, :].astype(F32), (8, LANES))
                part = pltpu.roll(part, shift + 64 * h, 1)
                parts.append(pltpu.roll(part, 0, 1, stride=8, stride_axis=0))
            return jnp.concatenate(parts, axis=0)

        lane = iota((16, LANES), 1)
        return jnp.where(lane < WEST, tall(west, 8), tall(east, 8 + WEST))[first : first + count]

    def prepare(k, slot):
        stage = stages.at[slot]
        spread = spreads.at[slot]
        dense = denses.at[slot]
        lane = iota((32, LANES), 1)
        for c in range(2):
            above = above_ref[k, 8 * c : 8 * c + 8, :].astype(F32)
            below = below_ref[k, 8 * c : 8 * c + 8, :].astype(F32)
            own = wind_ref[c, k].astype(F32)
            turned = pltpu.roll(jnp.concatenate([above, own, below], axis=0), WEST, 1)
            halo = jnp.concatenate(
                [
                    edge(above_ref[k, 16:24, :LANES], above_ref[k, 16:24, LANES : 2 * LANES], c, 8, 8),
                    edge(west_ref[k], east_ref[k], c, 0, 16),
                    edge(below_ref[k, 16:24, :LANES], below_ref[k, 16:24, LANES : 2 * LANES], c, 0, 8),
                ],
                axis=0,
            )
            first = turned[:, :LANES]
            extended = jnp.concatenate(
                [
                    jnp.where(lane < WEST, halo, first),
                    turned[:, LANES:],
                    jnp.where(lane < WEST, first, jnp.where(lane < 15, halo, 0.0)),
                ],
                axis=1,
            )
            for b in range(4):
                moved = extended if b == 0 else pltpu.roll(extended, cols + LANES - b, 1)
                for t in range(cols // LANES + 1):
                    stage[t, pl.ds(2 * b + c, 32, stride=8), :] = moved[:, LANES * t : LANES * (t + 1)]
        for t in range(cols // LANES + 1):
            spread[:, LANES * t : LANES * (t + 1)] = stage[t].astype(BF16)

        row_off = cells_ref[0, k]
        col_off = cells_ref[1, k]
        row_mid = row_off >> 1
        col_mid = col_off >> 1
        for t in range(cols // LANES):
            dense[t, 0:16, :] = (col_mid[:, LANES * t : LANES * (t + 1)] + 6).astype(F32)
            dense[t, 16:32, :] = (row_mid[:, LANES * t : LANES * (t + 1)] + 4).astype(F32)

    def collect(slot):
        spread = spreads.at[slot]
        dense = denses.at[slot]
        taps = tapss.at[slot]
        def gather(pair, carry):
            y = 2 * pair
            start = pl.multiple_of(16 * pair + 16, 16)
            for block in range(cols // LANES):
                lo = block * LANES
                halves = []
                for n in range(2):
                    at = dense[block, pl.ds(y + n, 8, stride=0), :]
                    at = jnp.concatenate([at, at], axis=0)
                    halves.append(jnp.where(lane_pos[...] == at, 1.0, 0.0))
                compact = jnp.concatenate(halves, axis=1).astype(BF16)
                found = jnp.dot(
                    spread[pl.ds(start, 112), lo : lo + 256],
                    band_matrix(compact, mask),
                    preferred_element_type=F32,
                )
                for n in range(2):
                    depth = dense[block, pl.ds(16 + y + n, 8, stride=0), :]
                    v = [
                        found[8 * (1 + n + i) : 8 * (2 + n + i), n * LANES : (n + 1) * LANES]
                        for i in range(12)
                    ]
                    whole = depth >= 8.0
                    v = [jnp.where(whole, v[i + 8], v[i]) for i in range(4)] + v[4:]
                    depth = jnp.where(whole, depth - 8.0, depth)
                    for step, count in ((4, 7), (2, 5), (1, 4)):
                        far = depth >= float(step)
                        v = [jnp.where(far, v[i + step], v[i]) for i in range(count)]
                        depth = jnp.where(far, depth - float(step), depth)
                    for a in range(4):
                        taps[block, pl.ds(a * 136 + y + n, 8, stride=17), :] = v[a]
            return carry

        for pair in range(rows // 2):
            gather(pair, 0)

    def iterate(k, slot):
        taps = tapss.at[slot]
        row_off = cells_ref[0, k]
        col_off = cells_ref[1, k]
        for half in range(rows // 8):
            for tile in range(cols // LANES):
                rr = slice(8 * half, 8 * half + 8)
                cc = slice(LANES * tile, LANES * tile + LANES)
                cy = param_ref[16:24, :]
                dy = param_ref[24:32, :]
                dx = param_ref[32:40, :]
                cx = param_ref[rr, :]
                oy = row_off[rr, cc]
                ox = col_off[rr, cc]
                y_odd = (oy & 1).astype(F32)
                x_odd = (ox & 1).astype(F32)
                oyf = oy.astype(F32) + 0.5
                oxf = ox.astype(F32) + 0.5
                fy = jnp.full((8, LANES), 0.5, F32)
                fx = fy
                for _ in range(ITERS):
                    wy = cubic_weights((y_odd + fy) * 0.5)
                    wx = [w.astype(BF16).astype(F32) for w in cubic_weights((x_odd + fx) * 0.5)]
                    mid = []
                    for c in range(2):
                        total = None
                        for a in range(4):
                            along = None
                            for b in range(4):
                                base = a * 136 + (2 * b + c) * 17 + 8 * half
                                term = wx[b] * taps[tile, base : base + 8, :]
                                along = term if along is None else along + term
                            along = wy[a] * along
                            total = along if total is None else total + along
                        mid.append(total)
                    lx = dx * jnp.tanh(mid[0] * cx)
                    ly = dy * jnp.tanh(mid[1] * cy)
                    fy = 0.5 + 0.5 * jnp.tanh(0.5 * (ly - oyf))
                    fx = 0.5 + 0.5 * jnp.tanh(0.5 * (lx - oxf))
                row_frac_ref[k, rr, cc] = fy
                col_frac_ref[k, rr, cc] = fx

    def track_levels(group, carry):
        for slot in range(SLOTS):
            prepare(SLOTS * group + slot, slot)
        for slot in range(SLOTS):
            collect(slot)
            iterate(SLOTS * group + slot, slot)
        return carry

    lax.fori_loop(0, levels // SLOTS, track_levels, 0)


def advect_kernel(
    own_ref, above_ref, below_ref, west_ref, east_ref, far_above_ref, far_below_ref, cells_ref,
    row_frac_ref, col_frac_ref,
    out_ref,
    spreads, mask, lane_pos, denses, results,
):
    channels, levels, rows, cols = out_ref.shape
    fill_band_tables(mask, lane_pos)

    def place(spread, block, west, east, first, count, at):
        west = west.astype(F32)
        east = east.astype(F32)
        halo = []
        lane = iota((8, LANES), 1)
        for r in range(first, first + count):
            a = pltpu.roll(west, (8 * r + 8) % LANES, 1)
            b = pltpu.roll(east, (8 * r + 8 + WEST) % LANES, 1)
            halo.append(jnp.where(lane < WEST, a, jnp.where(lane < 15, b, 0.0)))
        halo = jnp.concatenate(halo, axis=0)
        lanes = iota((8 * count, LANES), 1)
        start = block[:, :LANES].astype(F32)
        spread[at : at + 8 * count, :LANES] = jnp.where(lanes < WEST, halo, start).astype(BF16)
        spread[at : at + 8 * count, LANES:cols] = block[:, LANES:]
        spread[at : at + 8 * count, cols:] = jnp.where(lanes < WEST, start, halo).astype(BF16)

    def prepare(k, slot):
        spread = spreads.at[slot]
        dense = denses.at[slot]
        place(spread, above_ref[k], far_above_ref[k, 16:24, :LANES], far_above_ref[k, 16:24, LANES : 2 * LANES], rows - HL, HL, 0)
        place(spread, own_ref[k], west_ref[k], east_ref[k], 0, rows, 8 * HL)
        place(spread, below_ref[k], far_below_ref[k, 16:24, :LANES], far_below_ref[k, 16:24, LANES : 2 * LANES], 0, HL, 8 * (HL + rows))

        for t in range(cols // LANES):
            cc = slice(LANES * t, LANES * (t + 1))
            dense[t, 0:16, :] = (cells_ref[1, k, :, cc] + 6).astype(F32)
            dense[t, 16:32, :] = (cells_ref[0, k, :, cc] + 8).astype(F32)
            for i, w in enumerate(cubic_weights(col_frac_ref[k, :, cc])):
                dense[t, 32 + 16 * i : 48 + 16 * i, :] = w.astype(BF16).astype(F32)
            for i, w in enumerate(cubic_weights(row_frac_ref[k, :, cc])):
                dense[t, 96 + 16 * i : 112 + 16 * i, :] = w

    def collect(k, slot):
        spread = spreads.at[slot]
        dense = denses.at[slot]
        result = results.at[slot]
        def sample(pair, carry):
            y = 2 * pair
            start = pl.multiple_of(16 * pair, 16)
            for block in range(cols // LANES):
                lo = block * LANES
                halves = []
                for n in range(2):
                    def wide(part):
                        return dense[block, pl.ds(16 * part + y + n, 8, stride=0), :]

                    at = wide(0)
                    w = [wide(2 + b) for b in range(4)]
                    both = []
                    for h in range(2):
                        rel = lane_pos[8 * h : 8 * h + 8, :] - at
                        picked = jnp.where(rel == 3.0, w[3], 0.0)
                        picked = jnp.where(rel == 2.0, w[2], picked)
                        picked = jnp.where(rel == 1.0, w[1], picked)
                        both.append(jnp.where(rel == 0.0, w[0], picked))
                    halves.append(jnp.concatenate(both, axis=0))
                compact = jnp.concatenate(halves, axis=1).astype(BF16)
                mixed = jnp.dot(
                    spread[pl.ds(start, 176), lo : lo + 256],
                    band_matrix(compact, mask),
                    preferred_element_type=F32,
                )
                for n in range(2):
                    depth = dense[block, pl.ds(16 + y + n, 8, stride=0), :]
                    v = [
                        mixed[8 * (1 + n + i) : 8 * (2 + n + i), n * LANES : (n + 1) * LANES]
                        for i in range(20)
                    ]
                    whole = depth >= 16.0
                    v = [jnp.where(whole, v[i + 16], v[i]) for i in range(4)] + v[4:]
                    depth = jnp.where(whole, depth - 16.0, depth)
                    for step, count in ((8, 11), (4, 7), (2, 5), (1, 4)):
                        far = depth >= float(step)
                        v = [jnp.where(far, v[i + step], v[i]) for i in range(count)]
                        depth = jnp.where(far, depth - float(step), depth)
                    total = None
                    for a in range(4):
                        weight = dense[block, pl.ds(96 + 16 * a + y + n, 8, stride=0), :]
                        total = weight * v[a] if total is None else total + weight * v[a]
                    result[block, pl.ds(y + n, 8, stride=17), :] = total
            return carry

        for pair in range(rows // 2):
            sample(pair, 0)
        for c in range(channels):
            for t in range(cols // LANES):
                cc = slice(LANES * t, LANES * (t + 1))
                out_ref[c, k, :, cc] = result[t, 17 * c : 17 * c + 16, :].astype(BF16)

    def advect_levels(group, carry):
        for slot in range(SLOTS):
            prepare(SLOTS * group + slot, slot)
        for slot in range(SLOTS):
            collect(SLOTS * group + slot, slot)
        return carry

    lax.fori_loop(0, levels // SLOTS, advect_levels, 0)


def call(kernel, outs, scratch, args, name, flops):
    moved = sum(a.size * a.dtype.itemsize for a in list(args) + list(outs))
    in_vmem = pl.BlockSpec(memory_space=pltpu.VMEM)
    return pl.pallas_call(
        kernel,
        in_specs=[pl.BlockSpec(memory_space=pltpu.SMEM) if a.size == 2 else in_vmem for a in args],
        out_specs=[in_vmem] * len(outs),
        out_shape=outs,
        scratch_shapes=scratch,
        cost_estimate=pl.CostEstimate(flops=flops, bytes_accessed=moved, transcendentals=0),
        compiler_params=pltpu.CompilerParams(vmem_limit_bytes=24 << 20),
        name=name,
    )(*args)


def on_device(prognostic, halo_depth, cell_offsets):
    channels, levels, rows, cols = prognostic.shape
    tiles = cols // LANES
    shape = jax.ShapeDtypeStruct
    edge = shape((levels, 8, LANES), BF16)
    edge_west, edge_east = call(
        edge_kernel, [edge, edge], [pltpu.VMEM((8 * rows, LANES), F32)], [prognostic], "edge", 10**6
    )
    west = from_behind(edge_east, "lon", 1)
    east = from_behind(edge_west, "lon", -1)
    own, down, up = call(
        pack_kernel,
        [shape((levels, 8 * n, cols), BF16) for n in (rows, HL, HL)],
        [pltpu.VMEM((tiles, 8 * rows, LANES), F32)],
        [prognostic], "pack", 10**6,
    )

    edges = jnp.concatenate([west, east, jnp.zeros((levels, 8, cols - 2 * LANES), BF16)], axis=2)
    send_down = jnp.concatenate([prognostic[0, :, rows - 8 :], prognostic[1, :, rows - 8 :], edges], axis=1)
    send_up = jnp.concatenate([prognostic[0, :, :8], prognostic[1, :, :8], edges], axis=1)
    send_down, send_up = lax.optimization_barrier((send_down, send_up))
    far_above = passed_along(send_down, "lat", 1)
    far_below = passed_along(send_up, "lat", -1)
    above = passed_along(down, "lat", 1)
    below = passed_along(up, "lat", -1)

    frac = shape((levels, rows, cols), F32)
    row_frac, col_frac = call(
        track_kernel,
        [frac, frac],
        [
            pltpu.VMEM((SLOTS, tiles + 1, 8 * 32, LANES), F32),
            pltpu.VMEM((SLOTS, 8 * 32, cols + LANES), BF16),
            pltpu.VMEM((144, 256), BF16),
            pltpu.VMEM((16, LANES), F32),
            pltpu.VMEM((SLOTS, tiles, 32, LANES), F32),
            pltpu.VMEM((SLOTS, tiles, 4 * 136, LANES), F32),
            pltpu.VMEM((rows + 24, LANES), F32),
        ],
        [prognostic, far_above, far_below, west, east, cell_offsets, halo_depth],
        "track", 10**10,
    )
    return call(
        advect_kernel,
        [shape(prognostic.shape, BF16)],
        [
            pltpu.VMEM((SLOTS, 8 * (rows + 2 * HL), cols + LANES), BF16),
            pltpu.VMEM((144, 256), BF16),
            pltpu.VMEM((16, LANES), F32),
            pltpu.VMEM((SLOTS, tiles, 160, LANES), F32),
            pltpu.VMEM((SLOTS, tiles, 136, LANES), F32),
        ],
        [own, above, below, west, east, far_above, far_below, cell_offsets, row_frac, col_frac],
        "advect", 40 * 10**6,
    )[0]


def solution(mesh):
    in_specs = (P(None, None, "lat", "lon"), P(None, "lat", "lon"), P(None, None, "lat", "lon"))
    out_specs = P(None, None, "lat", "lon")
    return jax.shard_map(
        on_device, mesh=mesh, in_specs=in_specs, out_specs=out_specs, check_vma=False
    )
```
